256 devices in a mesh: grp: 8 (over z), ord: 32 (over x, y, core).
Axes of the slice: x: 4, y: 4, z: 8, core: 2. Of those that a mesh axis runs over, the one named last changes fastest.
Arguments:
- legendre: float32 [512, 1048576], P('ord', 'grp')
- lon_center: float32 [8], P('grp'), may hold values from 0 to 1
- counts: int32 [8, 32], P('grp'), may hold values from 1 to 4096, 98304 in all within a row
- column_index: int32 [3, 512], replicated, may hold values from 0 to 120, as said below
Outputs:
- factor: float32 [512, 512], replicated
The draws below stay inside these ranges and needn't reach their ends.
Inputs may be any that keep to these rules, and one draw needn't show every extreme that they name: `column_index`: each column names a different coefficient: row 0 is its degree (at most 120), row 1 its order (at most the degree), row 2 is 1 for a sine term and 0 for a cosine term, and 0 at order 0. Each group's counts add up to 98304.
All inputs are finite; a program needn't handle non-finite values.
Results may differ from the reference program's by a relative error of at most 0.0003.
Values sent between devices are 32-bit elements; how exact they have to be, the bound alone decides.
A program may use at most 64 MiB of HBM per device.

```python
import math
import jax
import jax.numpy as jnp
import numpy as np
from jax import lax

NMAX = 120
COLS = 512
ROWS_DEV = 4096
ROWS_GRP = 131072
ROWS = 1048576
N_GRP = 8
N_ORD = 32


def draw_legendre(key, part):
    key_rough, key_common, key_column, key_shared = jax.random.split(key, 4)
    rough_part = jax.random.normal(key_rough, (COLS, ROWS), jnp.float32)
    common_row = jax.random.normal(key_common, (ROWS,), jnp.float32)
    column_gain = jnp.exp(jax.random.uniform(key_column, (COLS,), jnp.float32, -0.693, 0.693))
    common_gain = jax.random.uniform(key_shared, (COLS,), jnp.float32, 0.4, 1.2)
    position = jnp.arange(ROWS, dtype=jnp.float32) / (ROWS - 1)
    row_scale = 0.5 + position
    mixed = rough_part + common_gain[:, None] * common_row[None, :]
    return column_gain[:, None] * row_scale[None, :] * mixed


def draw_column_index(key, part):
    entries = []
    for degree in range(NMAX + 1):
        for harmonic_order in range(degree + 1):
            flags = (0,) if harmonic_order == 0 else (0, 1)
            for sine_flag in flags:
                entries.append((degree, harmonic_order, sine_flag))
    lookup = jnp.asarray(np.array(entries, dtype=np.int32).T)
    chosen = jax.random.permutation(key, lookup.shape[1])[:COLS]
    return lookup[:, chosen].astype(jnp.int32)


def levels(own_key, extent, shards, least, high):
    factor_of = 1.0
    for dim, parts in shards:
        steps = jax.random.uniform(jax.random.fold_in(jax.random.fold_in(own_key, 6), dim), (parts,), jnp.float32, least / len(shards), high / len(shards))
        factor_of = factor_of * jnp.repeat(jnp.exp(steps), extent[dim] // parts).reshape((-1,) + (1,) * (len(extent) - 1 - dim))
    return factor_of


def length_profile(amount, total, limit, skew):
    loads = [(1 << 20) // math.isqrt(rank ** skew) + 1 for rank in range(2, amount + 1)]
    spare, given = total - limit - (amount - 1), [1] * (amount - 1)
    while spare > 0:
        free = [i for i in range(amount - 1) if given[i] < limit]
        pool, left = sum([loads[i] for i in free]), spare
        for i in free:
            addition = min(limit - given[i], max(1, left * loads[i] // pool), spare)
            given[i] = given[i] + addition
            spare = spare - addition
    return np.array([limit] + given)


def ragged_sizes(own_key, number_of, total, bound, slope):
    if number_of == 2:
        one = jax.random.randint(own_key, (), max(1, total - bound), min(bound, total - 1) + 1)
        return jnp.stack([one, total - one])
    tallies = jnp.asarray(length_profile(number_of, total, bound, slope), jnp.int32)
    couples = (number_of - 1) // 2
    donor, sink = tallies[1:1 + 2 * couples:2], tallies[2:2 + 2 * couples:2]
    slack = jnp.minimum(donor - 1, bound - sink)
    moved = jax.random.randint(jax.random.fold_in(own_key, 1), (couples,), 0, 1 << 20) % (slack + 1)
    tallies = tallies.at[1:1 + 2 * couples:2].set(donor - moved).at[2:2 + 2 * couples:2].set(sink + moved)
    return tallies[jax.random.permutation(jax.random.fold_in(own_key, 2), number_of)]


def setup_inputs(seed: int = 0) -> dict:
    key_of = jax.random.split(jax.random.key(seed), 5)
    return {
        "legendre": draw_legendre(jax.random.fold_in(key_of[4], 71), 0),
        "lon_center": jnp.clip(1.0 * jax.random.uniform(key_of[1], (N_GRP,), jnp.float32) ** levels(key_of[1], (N_GRP,), ((0, 8),), -0.2, 0.2), 0.0, 1.0),
        "counts": jax.vmap(lambda own: ragged_sizes(own, N_ORD, N_ORD * ROWS_DEV * 3 // 4, ROWS_DEV, 2))(jax.random.split(key_of[2], N_GRP)).reshape((N_GRP, N_ORD)).astype(jnp.int32),
        "column_index": draw_column_index(jax.random.fold_in(key_of[4], 71), 0),
    }


quarter_turn = math.pi / 2
track_span = 0.3
kaula_gain = 1.2

def reference(legendre, lon_center, counts, column_index):
    harmonic = column_index[1].astype(jnp.float32)
    sine_part = column_index[2].astype(jnp.float32)
    along = jnp.arange(ROWS_GRP, dtype=jnp.float32) * (track_span / ROWS_GRP)
    slot_index = jnp.arange(ROWS_DEV, dtype=jnp.int32)
    scaling = 1.0 / math.sqrt(ROWS)

    def one_group(total, group):
        start = (group * ROWS_GRP).astype(jnp.int32)
        rows_block = lax.dynamic_slice_in_dim(legendre, start, ROWS_GRP, 1)
        longitude = lon_center[group] + along
        harmonic_wave = jnp.cos(harmonic[:, None] * longitude[None, :] - sine_part[:, None] * quarter_turn)
        row_valid = (slot_index[None, :] < counts[group][:, None]).astype(jnp.float32).reshape(ROWS_GRP)
        design = rows_block * harmonic_wave * (row_valid * scaling)[None, :]
        return (total + jnp.dot(design, design.T, precision=lax.Precision.HIGHEST), None)
    gram, _ = lax.scan(one_group, jnp.zeros((COLS, COLS), jnp.float32), jnp.arange(N_GRP, dtype=jnp.int32))
    degree = column_index[0].astype(jnp.float32)
    kaula_weight = kaula_gain * (degree / NMAX) ** 2
    normal = gram + jnp.diag(kaula_weight * kaula_weight)
    return jnp.linalg.cholesky(normal).T
```

```python
import math

import jax
import jax.numpy as jnp
import numpy as np
from jax import lax
from jax.experimental import pallas as pl
from jax.experimental.pallas import tpu as pltpu
from jax.sharding import PartitionSpec as P

NMAX = 120

track_span = 0.3
kaula_gain = 1.2
highest = lax.Precision.HIGHEST
by_mesh = pl.DeviceIdType.MESH

LANES = 128
TILE_BLOCKS = 4
UPPER = [(i, j) for i in range(TILE_BLOCKS) for j in range(i, TILE_BLOCKS)]

CHIP_OFFSETS = [
    (2, 2), (2, 1), (1, 2), (2, 3), (3, 2), (2, 0), (0, 2), (1, 1), (3, 3), (1, 3), (3, 1),
    (1, 0), (0, 1), (3, 0), (0, 3),
]
OFFSETS = [(dx, dy, dc) for dc in (0, 1) for dx, dy in CHIP_OFFSETS] + [(0, 0, 1)]
DEPTHS = (4, 3, 5, 2, 6, 1, 7)


def sine_terms():
    g = np.cos(np.linspace(0.0, np.pi / 2, 400)) * 0.25
    g = g[g > 1e-4]
    powers = np.stack([g ** (2 * k + 1) for k in range(6)], axis=1)
    return [float(c) for c in np.linalg.lstsq(powers, np.sin(2 * np.pi * g), rcond=None)[0]]


SINE = sine_terms()


def tiles_in(count):
    return lax.shift_right_logical(count + (LANES - 1), 7)


def compact_kernel(counts_ref, legendre_ref, out_ref, sem):
    segments = counts_ref.shape[1]
    per_segment = legendre_ref.shape[1] // segments // LANES
    sizes = [1 << b for b in reversed(range(per_segment.bit_length()))]

    def span(at, size):
        return pl.ds(pl.multiple_of(at * LANES, LANES), size * LANES)

    def segment(k, to):
        n = tiles_in(counts_ref[0, k])
        at = k * per_segment
        for size in sizes:
            has = (n & size) != 0

            @pl.when(has)
            def _(at=at, to=to, size=size):
                pltpu.make_async_copy(legendre_ref.at[:, span(at, size)], out_ref.at[:, span(to, size)], sem).start()

            step = jnp.where(has, size, 0)
            at, to = at + step, to + step
        return to

    moved = lax.fori_loop(0, segments, segment, jnp.int32(0))
    for b in reversed(range((out_ref.shape[1] // LANES).bit_length())):
        @pl.when((moved & (1 << b)) != 0)
        def _(b=b):
            whole = pl.ds(0, LANES << b)
            pltpu.make_async_copy(legendre_ref.at[:, whole], out_ref.at[:, whole], sem).wait()


def compact(legendre, counts, lanes):
    return pl.pallas_call(
        compact_kernel,
        out_shape=jax.ShapeDtypeStruct((legendre.shape[0], lanes), jnp.float32),
        in_specs=[pl.BlockSpec(memory_space=pltpu.SMEM), pl.BlockSpec(memory_space=pltpu.HBM)],
        out_specs=pl.BlockSpec(memory_space=pltpu.VMEM),
        scratch_shapes=[pltpu.SemaphoreType.DMA],
        compiler_params=pltpu.CompilerParams(vmem_limit_bytes=12 * 2**20),
        name="compact",
    )(counts, legendre)


def gram_kernel(rows_grp, width, lon_ref, counts_ref, index_ref, own_ref, out_ref,
                starts, tile_at, filled, order, first, got, high, low, packed, part, plane, piece, total,
                own_sem, send_sem, recv_sem, send1, recv1, send2, recv2, send3, recv3):
    me = lax.axis_index("ord")
    depth = lax.axis_index("grp")
    segments = counts_ref.shape[1]
    per_segment = rows_grp // segments // LANES
    chunks, _, cols, lanes = got.shape
    total_cols = segments * cols
    x, y, core = me // 8, (me // 2) % 4, me % 2

    def neighbour(offset):
        dx, dy, dc = offset
        return ((x + dx) % 4) * 8 + ((y + dy) % 4) * 2 + (core + dc) % 2

    peers = [neighbour(o) for o in OFFSETS]
    layers = [(depth + d) % 8 for d in DEPTHS]

    barrier = pltpu.get_barrier_semaphore()
    for peer in peers:
        pl.semaphore_signal(barrier, inc=1, device_id={"ord": peer}, device_id_type=by_mesh)
    for layer in layers:
        pl.semaphore_signal(barrier, inc=1, device_id={"grp": layer}, device_id_type=by_mesh)
    pl.semaphore_wait(barrier, len(peers) + len(layers))

    def own_tiles(c, d):
        return own_ref.at[:, pl.ds(pl.multiple_of((c * segments + d) * lanes, LANES), lanes)]

    def chunk_copy(c, j):
        return pltpu.make_async_remote_copy(
            src_ref=own_tiles(c, peers[j]), dst_ref=got.at[c, me], send_sem=send_sem.at[c, j],
            recv_sem=recv_sem.at[c, j], device_id={"ord": peers[j]}, device_id_type=by_mesh)

    def own_copy(c):
        return pltpu.make_async_copy(own_tiles(c, me), got.at[c, me], own_sem.at[c])

    def send_chunk(c, carry):
        for j in range(len(peers)):
            chunk_copy(c, j).start()
        own_copy(c).start()
        return carry

    lax.fori_loop(0, chunks, send_chunk, 0)

    begin = jnp.int32(0)
    for k in range(segments):
        starts[k] = begin
        begin = begin + tiles_in(counts_ref[0, k])

    def list_tile(t, carry):
        at = (t // width * segments + me) * width + t % width
        tile, left = jnp.int32(0), jnp.int32(0)
        for k in range(segments):
            step = at - starts[k]
            left_here = counts_ref[0, k] - step * LANES
            inside = jnp.logical_and(step >= 0, left_here > 0)
            tile = jnp.where(inside, k * per_segment + step, tile)
            left = jnp.where(inside, left_here, left)
        tile_at[t] = tile
        filled[t] = left
        return carry

    lax.fori_loop(0, chunks * width, list_tile, 0)

    rate = track_span / rows_grp / (2 * math.pi)
    start = lon_ref[0] * (1.0 / (2 * math.pi))
    for i in range(TILE_BLOCKS):
        mine = slice(i * LANES, (i + 1) * LANES)

        def down(row):
            return jnp.transpose(jnp.broadcast_to(index_ref[row:row + 1, mine], (LANES, LANES)).astype(jnp.float32))

        m = down(1)
        base = m * start - 0.25 * down(2)
        base = base - jnp.floor(base + 0.5)
        order[mine, :] = m
        first[mine, :] = base + m * (rate * lax.broadcasted_iota(jnp.int32, (LANES, LANES), 1).astype(jnp.float32))
    scale = 1.0 / math.sqrt(rows_grp * lax.axis_size("grp"))
    packed[...] = jnp.zeros_like(packed)

    def product(left, right):
        return lax.dot_general(left, right, (((1,), (1,)), ((), ())), preferred_element_type=jnp.float32)

    def add_chunk(c, carry):
        for j in range(len(peers)):
            chunk_copy(c, j).wait_recv()
        own_copy(c).wait()
        for i in range(width):
            t = c * width + i
            shift = tile_at[t].astype(jnp.float32) * (rate * LANES)
            count = filled[t]
            part_lanes = slice(i * LANES, (i + 1) * LANES)

            def wave_rows(r, carry):
                rows = pl.ds(pl.multiple_of(r * 64, 64), 64)
                values = got[c, pl.ds(r * (64 // cols), 64 // cols), :, part_lanes].reshape(64, LANES)
                turns = first[rows, :] + order[rows, :] * shift
                turns = turns - jnp.floor(turns + 0.5)
                g = 0.25 - jnp.abs(turns)
                z = g * g
                wave = jnp.full_like(z, SINE[-1] * scale)
                for term in SINE[-2::-1]:
                    wave = wave * z + term * scale
                lane = lax.broadcasted_iota(jnp.int32, (64, LANES), 1)
                values = jnp.where(lane < count, values * (wave * g), 0.0)
                upper = values.astype(jnp.bfloat16)
                high[rows, part_lanes] = upper
                low[rows, part_lanes] = (values - upper.astype(jnp.float32)).astype(jnp.bfloat16)
                return carry

            lax.fori_loop(0, total_cols // 64, wave_rows, 0)
        at = 0
        for i in range(TILE_BLOCKS):
            mine = slice(i * LANES, (i + 1) * LANES)
            rest = slice(i * LANES, total_cols)
            gram = product(high[mine, :], high[rest, :])
            gram += product(high[mine, :], low[rest, :])
            gram += product(low[mine, :], high[rest, :])
            for k in range(TILE_BLOCKS - i):
                packed[at * LANES:(at + 1) * LANES, :] += gram[:, k * LANES:(k + 1) * LANES]
                at += 1
        return carry

    lax.fori_loop(0, chunks, add_chunk, 0)

    share = piece.shape[0]

    def rows_of(d):
        return pl.ds(pl.multiple_of(d * share, 8), share)

    first_step = [
        pltpu.make_async_remote_copy(
            src_ref=packed.at[rows_of(peers[j])], dst_ref=part.at[j], send_sem=send1.at[j], recv_sem=recv1.at[j],
            device_id={"ord": peers[j]}, device_id_type=by_mesh)
        for j in range(len(peers))
    ]
    for copy in first_step:
        copy.start()
    value = packed[rows_of(me), :]
    for j, copy in enumerate(first_step):
        copy.wait_recv()
        value = value + part[j]
    plane[depth] = value
    second_step = [
        pltpu.make_async_remote_copy(
            src_ref=plane.at[depth], dst_ref=plane.at[depth], send_sem=send2.at[j], recv_sem=recv2.at[j],
            device_id={"grp": layers[j]}, device_id_type=by_mesh)
        for j in range(len(layers))
    ]
    for copy in second_step:
        copy.start()
    for copy in second_step:
        copy.wait_recv()
    value = plane[0]
    for d in range(1, 8):
        value = value + plane[d]
    piece[...] = value
    third_step = [
        pltpu.make_async_remote_copy(
            src_ref=piece, dst_ref=total.at[rows_of(me)], send_sem=send3.at[j], recv_sem=recv3.at[j],
            device_id={"ord": peers[j]}, device_id_type=by_mesh)
        for j in range(len(peers))
    ]
    for copy in third_step:
        copy.start()
    total[rows_of(me), :] = value
    for copy in third_step:
        copy.wait_recv()
    out_ref[...] = total[...]
    for copy in first_step + second_step + third_step:
        copy.wait_send()

    def drain(c, carry):
        for j in range(len(peers)):
            chunk_copy(c, j).wait_send()
        return carry

    lax.fori_loop(0, chunks, drain, 0)


def panel_gram(legendre, lon_center, counts, column_index):
    cols, rows_grp = legendre.shape
    segments = counts.shape[1]
    total_cols = column_index.shape[1]
    tiles = (rows_grp * 3 // 4) // LANES + segments
    width = 5
    chunks = -(-tiles // (segments * width))
    packed_rows = len(UPPER) * LANES
    share = packed_rows // segments
    peers, layers = len(OFFSETS), len(DEPTHS)
    f32 = jnp.float32
    dma = pltpu.SemaphoreType.DMA
    own = compact(legendre, counts, chunks * segments * width * LANES)
    return pl.pallas_call(
        lambda *refs: gram_kernel(rows_grp, width, *refs),
        out_shape=jax.ShapeDtypeStruct((packed_rows, LANES), f32),
        in_specs=[
            pl.BlockSpec(memory_space=pltpu.SMEM),
            pl.BlockSpec(memory_space=pltpu.SMEM),
            pl.BlockSpec(memory_space=pltpu.VMEM),
            pl.BlockSpec(memory_space=pl.ANY),
        ],
        out_specs=pl.BlockSpec(memory_space=pltpu.VMEM),
        scratch_shapes=[
            pltpu.SMEM((segments,), jnp.int32),
            pltpu.SMEM((chunks * width,), jnp.int32),
            pltpu.SMEM((chunks * width,), jnp.int32),
            pltpu.VMEM((total_cols, LANES), f32),
            pltpu.VMEM((total_cols, LANES), f32),
            pltpu.VMEM((chunks, segments, cols, width * LANES), f32),
            pltpu.VMEM((total_cols, width * LANES), jnp.bfloat16),
            pltpu.VMEM((total_cols, width * LANES), jnp.bfloat16),
            pltpu.VMEM((packed_rows, LANES), f32),
            pltpu.VMEM((peers, share, LANES), f32),
            pltpu.VMEM((layers + 1, share, LANES), f32),
            pltpu.VMEM((share, LANES), f32),
            pltpu.VMEM((packed_rows, LANES), f32),
            dma((chunks,)),
            dma((chunks, peers)), dma((chunks, peers)),
            dma((peers,)), dma((peers,)),
            dma((layers,)), dma((layers,)),
            dma((peers,)), dma((peers,)),
        ],
        compiler_params=pltpu.CompilerParams(collective_id=0, has_side_effects=True, vmem_limit_bytes=24 * 2**20),
        name="panel_gram",
    )(lon_center, counts, column_index, own)


def lane_spread(v, j):
    return jnp.broadcast_to(v[:, j:j + 1], (8, 128))


def row_spread(v, i):
    return jnp.broadcast_to(v[i:i + 1, :], (8, 128))


def tree(terms):
    terms = list(terms)
    while len(terms) > 1:
        terms = [terms[i] + terms[i + 1] if i + 1 < len(terms) else terms[i] for i in range(0, len(terms), 2)]
    return terms[0]


def panel(a, out, k, p, tiles):
    base = 128 * k if isinstance(k, int) else pl.multiple_of(128 * k, 128)
    def cols(t):
        return pl.ds(base + 128 * t, 128)
    row = base + 8 * p
    sub = lax.broadcasted_iota(jnp.int32, (8, 128), 0)
    lane = lax.broadcasted_iota(jnp.int32, (8, 128), 1)
    rows = [a[pl.ds(row, 8), cols(t)] for t in range(tiles)]
    spread = [lane_spread(rows[0], 8 * p + j) for j in range(8)]
    e = {(i, j): row_spread(spread[j], i) for j in range(8) for i in range(j + 1)}
    m = {}
    n = {}
    for i in range(8):
        d = e[i, i]
        r = 1.0 / d
        s = lax.rsqrt(d)
        fac = {j: e[i, j] * r for j in range(i + 1, 8)}
        for j in range(i + 1, 8):
            for q in range(j, 8):
                e[j, q] = e[j, q] - fac[j] * e[i, q]
        for j in range(i + 1, 8):
            for c in range(i):
                m[j, c] = m[j, c] - fac[j] * m[i, c]
            m[j, i] = -fac[j]
        for c in range(i):
            n[i, c] = s * m[i, c]
        n[i, i] = s
    mcol = []
    for c in range(8):
        acc = jnp.zeros((8, 128), jnp.float32)
        for i in range(c, 8):
            acc = jnp.where(sub == i, n[i, c], acc)
        mcol.append(acc)
    pb = [[row_spread(rows[t], c) for c in range(8)] for t in range(tiles)]
    new = [tree(mcol[c] * pb[t][c] for c in range(8)) for t in range(tiles)]
    for t in range(tiles):
        val = new[t] if t else jnp.where(lane >= 8 * p + sub, new[0], 0.0)
        out[pl.ds(row, 8), cols(t)] = val
    if p == 15:
        return
    nb = [None] * tiles
    nb[0] = [tree(n[i, c] * pb[0][c] for c in range(i + 1)) for i in range(8)]
    for t in range(1, tiles):
        nb[t] = [row_spread(new[t], i) for i in range(8)]
    turned = jnp.transpose(new[0]) if p < 14 else None
    for q in range(p + 1, 16):
        grow = base + 8 * q
        g = [a[pl.ds(grow, 8), cols(t)] for t in range(tiles)]
        if q == p + 1:
            gc = [lane_spread(g[0], 8 * p + c) for c in range(8)]
            h = [tree(n[i, c] * gc[c] for c in range(i + 1)) for i in range(8)]
        else:
            tt = turned[8 * q:8 * q + 8, :]
            h = [jnp.broadcast_to(tt[:, i:i + 1], (8, 128)) for i in range(8)]
        for t in range(tiles):
            a[pl.ds(grow, 8), cols(t)] = g[t] - tree(h[i] * nb[t][i] for i in range(8))


def factor_kernel(index_ref, packed_ref, out, a):
    n = a.shape[0]
    out[...] = jnp.zeros((n, n), jnp.float32)
    degree = index_ref[0:1, :].astype(jnp.float32)
    kaula = kaula_gain * (degree / NMAX) ** 2
    diagonal = lax.broadcasted_iota(jnp.int32, (LANES, LANES), 0) == lax.broadcasted_iota(jnp.int32, (LANES, LANES), 1)
    for at, (i, j) in enumerate(UPPER):
        block = packed_ref[at * LANES:(at + 1) * LANES, :]
        if i == j:
            weight = kaula[:, i * LANES:(i + 1) * LANES]
            block = block + jnp.where(diagonal, weight * weight, 0.0)
        a[i * LANES:(i + 1) * LANES, j * LANES:(j + 1) * LANES] = block
    for k in range(TILE_BLOCKS):
        for p in range(16):
            panel(a, out, k, p, TILE_BLOCKS - k)
        done = slice(k * LANES, (k + 1) * LANES)
        for i in range(k + 1, TILE_BLOCKS):
            left = out[done, i * LANES:(i + 1) * LANES]
            a[i * LANES:(i + 1) * LANES, i * LANES:] -= lax.dot_general(
                left, out[done, i * LANES:], (((0,), (0,)), ((), ())), precision=highest,
                preferred_element_type=jnp.float32)


def upper_factor(packed, column_index):
    n = column_index.shape[1]
    return pl.pallas_call(
        factor_kernel,
        out_shape=jax.ShapeDtypeStruct((n, n), jnp.float32),
        in_specs=[pl.BlockSpec(memory_space=pltpu.VMEM)] * 2,
        out_specs=pl.BlockSpec(memory_space=pltpu.VMEM),
        scratch_shapes=[pltpu.VMEM((n, n), jnp.float32)],
        compiler_params=pltpu.CompilerParams(vmem_limit_bytes=16 * 2**20),
        name="upper_factor",
    )(column_index, packed)


def body(legendre, lon_center, counts, column_index):
    packed = panel_gram(legendre, lon_center, counts, column_index)
    return upper_factor(packed, column_index)


def solution(mesh):
    placed = (P("ord", "grp"), P("grp"), P("grp", None), P())
    return jax.shard_map(body, mesh=mesh, in_specs=placed, out_specs=P(), check_vma=False)
```

```python
import math

import jax
import jax.numpy as jnp
import numpy as np
from jax import lax
from jax.experimental import pallas as pl
from jax.experimental.pallas import tpu as pltpu
from jax.sharding import PartitionSpec as P

NMAX = 120

track_span = 0.3
kaula_gain = 1.2
highest = lax.Precision.HIGHEST
by_mesh = pl.DeviceIdType.MESH

LANES = 128
TILE_BLOCKS = 4
UPPER = [(i, j) for i in range(TILE_BLOCKS) for j in range(i, TILE_BLOCKS)]

CHIP_OFFSETS = [
    (2, 2), (2, 1), (1, 2), (2, 3), (3, 2), (2, 0), (0, 2), (1, 1), (3, 3), (1, 3), (3, 1),
    (1, 0), (0, 1), (3, 0), (0, 3),
]
OFFSETS = [(dx, dy, dc) for dc in (0, 1) for dx, dy in CHIP_OFFSETS] + [(0, 0, 1)]
DEPTHS = (4, 3, 5, 2, 6, 1, 7)
SPANS = (24, 16)


def sine_terms():
    g = np.cos(np.linspace(0.0, np.pi / 2, 400)) * 0.25
    g = g[g > 1e-4]
    powers = np.stack([g ** (2 * k + 1) for k in range(6)], axis=1)
    return [float(c) for c in np.linalg.lstsq(powers, np.sin(2 * np.pi * g), rcond=None)[0]]


SINE = sine_terms()


def remote(src, dst, sems, index, device):
    return pltpu.make_async_remote_copy(src_ref=src, dst_ref=dst, send_sem=sems[0].at[index], recv_sem=sems[1].at[index],
                                        device_id=device, device_id_type=by_mesh)


def reduce_everywhere(me, depth, packed, other, part, plane, piece, total, *sems):
    pair_sems, sems1, sems2, sems3, sems4 = [sems[2 * k:2 * k + 2] for k in range(5)]
    x, y, core = me // 8, (me // 2) % 4, me % 2
    partner = me + 1 - 2 * core
    chip = me // 2
    chips = [((x + dx) % 4) * 4 + (y + dy) % 4 for dx, dy in CHIP_OFFSETS]
    layers = [(depth + d) % 8 for d in DEPTHS]
    half_rows = other.shape[0]
    spans, at = [], 0
    for n in SPANS:
        spans.append((at, n))
        at += n
    def at_half(c, start, n):
        return pl.ds(pl.multiple_of(c * half_rows + start, 8), n)
    pair = []
    for s, (a, n) in enumerate(spans):
        pair.append(remote(packed.at[at_half(1 - core, a * 16, n * 16)], other.at[pl.ds(a * 16, n * 16)], pair_sems, s, {"ord": partner}))
    for copy in pair:
        copy.start()
    def rows(c, a, n):
        return a * 16 + c * n
    first, second, third, fourth = [], [], [], []
    for s, (a, n) in enumerate(spans):
        pair[s].wait_recv()
        mine = at_half(core, a * 16, n * 16)
        packed[mine, :] = packed[mine, :] + other[pl.ds(a * 16, n * 16), :]
        step = [remote(packed.at[at_half(core, rows(c, a, n), n)], part.at[j, pl.ds(a, n)], sems1, (s, j), {"ord": c * 2 + core}) for j, c in enumerate(chips)]
        for copy in step:
            copy.start()
        first.append(step)
    for s, (a, n) in enumerate(spans):
        value = packed[at_half(core, rows(chip, a, n), n), :]
        for j, copy in enumerate(first[s]):
            copy.wait_recv()
            value = value + part[j, pl.ds(a, n), :]
        plane[depth, pl.ds(a, n), :] = value
        step = [remote(plane.at[depth, pl.ds(a, n)], plane.at[depth, pl.ds(a, n)], sems2, (s, j), {"grp": l}) for j, l in enumerate(layers)]
        for copy in step:
            copy.start()
        second.append(step)
    for s, (a, n) in enumerate(spans):
        for copy in second[s]:
            copy.wait_recv()
        value = plane[0, pl.ds(a, n), :]
        for d in range(1, 8):
            value = value + plane[d, pl.ds(a, n), :]
        piece[pl.ds(a, n), :] = value
        home = at_half(core, rows(chip, a, n), n)
        step = [remote(piece.at[pl.ds(a, n)], total.at[home], sems3, (s, j), {"ord": c * 2 + core}) for j, c in enumerate(chips)]
        for copy in step:
            copy.start()
        third.append(step)
        keep = remote(piece.at[pl.ds(a, n)], total.at[home], sems4, (s, 15), {"ord": partner})
        keep.start()
        fourth.append([keep])
        total[home, :] = value
    back = [((x - dx) % 4) * 4 + (y - dy) % 4 for dx, dy in CHIP_OFFSETS]
    for s, (a, n) in enumerate(spans):
        for j in reversed(range(15)):
            third[s][j].wait_recv()
            spot = total.at[at_half(core, rows(back[j], a, n), n)]
            copy = remote(spot, spot, sems4, (s, j), {"ord": partner})
            copy.start()
            fourth[s].append(copy)
    for s in range(len(spans)):
        for copy in fourth[s]:
            copy.wait_recv()
    return pair + [c for group in first + second + third + fourth for c in group]


def tiles_in(count):
    return lax.shift_right_logical(count + (LANES - 1), 7)


def compact_kernel(counts_ref, legendre_ref, out_ref, sem):
    segments = counts_ref.shape[1]
    per_segment = legendre_ref.shape[1] // segments // LANES
    sizes = [1 << b for b in reversed(range(per_segment.bit_length()))]

    def span(at, size):
        return pl.ds(pl.multiple_of(at * LANES, LANES), size * LANES)

    def segment(k, to):
        n = tiles_in(counts_ref[0, k])
        at = k * per_segment
        for size in sizes:
            has = (n & size) != 0

            @pl.when(has)
            def _(at=at, to=to, size=size):
                pltpu.make_async_copy(legendre_ref.at[:, span(at, size)], out_ref.at[:, span(to, size)], sem).start()

            step = jnp.where(has, size, 0)
            at, to = at + step, to + step
        return to

    moved = lax.fori_loop(0, segments, segment, jnp.int32(0))
    for b in reversed(range((out_ref.shape[1] // LANES).bit_length())):
        @pl.when((moved & (1 << b)) != 0)
        def _(b=b):
            whole = pl.ds(0, LANES << b)
            pltpu.make_async_copy(legendre_ref.at[:, whole], out_ref.at[:, whole], sem).wait()


def compact(legendre, counts, lanes):
    return pl.pallas_call(
        compact_kernel,
        out_shape=jax.ShapeDtypeStruct((legendre.shape[0], lanes), jnp.float32),
        in_specs=[pl.BlockSpec(memory_space=pltpu.SMEM), pl.BlockSpec(memory_space=pltpu.HBM)],
        out_specs=pl.BlockSpec(memory_space=pltpu.VMEM),
        scratch_shapes=[pltpu.SemaphoreType.DMA],
        compiler_params=pltpu.CompilerParams(vmem_limit_bytes=44 * 2**20),
        name="compact",
    )(counts, legendre)


def gram_kernel(rows_grp, width, lon_ref, counts_ref, index_ref, own_ref, out_ref,
                starts, tile_at, filled, order, first, got, high, low, packed, other, part, plane, piece, total,
                own_sem, send_sem, recv_sem, *step_sems):
    me = lax.axis_index("ord")
    depth = lax.axis_index("grp")
    segments = counts_ref.shape[1]
    per_segment = rows_grp // segments // LANES
    chunks, _, cols, lanes = got.shape
    total_cols = segments * cols
    x, y, core = me // 8, (me // 2) % 4, me % 2

    def neighbour(offset):
        dx, dy, dc = offset
        return ((x + dx) % 4) * 8 + ((y + dy) % 4) * 2 + (core + dc) % 2

    peers = [neighbour(o) for o in OFFSETS]
    layers = [(depth + d) % 8 for d in DEPTHS]

    barrier = pltpu.get_barrier_semaphore()
    for peer in peers:
        pl.semaphore_signal(barrier, inc=1, device_id={"ord": peer}, device_id_type=by_mesh)
    for layer in layers:
        pl.semaphore_signal(barrier, inc=1, device_id={"grp": layer}, device_id_type=by_mesh)
    pl.semaphore_wait(barrier, len(peers) + len(layers))

    def own_tiles(c, d):
        return own_ref.at[:, pl.ds(pl.multiple_of((c * segments + d) * lanes, LANES), lanes)]

    def chunk_copy(c, j):
        return pltpu.make_async_remote_copy(
            src_ref=own_tiles(c, peers[j]), dst_ref=got.at[c, me], send_sem=send_sem.at[c, j],
            recv_sem=recv_sem.at[c, j], device_id={"ord": peers[j]}, device_id_type=by_mesh)

    def own_copy(c):
        return pltpu.make_async_copy(own_tiles(c, me), got.at[c, me], own_sem.at[c])

    def send_chunk(c, carry):
        for j in range(len(peers)):
            chunk_copy(c, j).start()
        own_copy(c).start()
        return carry

    lax.fori_loop(0, chunks, send_chunk, 0)

    begin = jnp.int32(0)
    for k in range(segments):
        starts[k] = begin
        begin = begin + tiles_in(counts_ref[0, k])

    def list_tile(t, carry):
        at = (t // width * segments + me) * width + t % width
        tile, left = jnp.int32(0), jnp.int32(0)
        for k in range(segments):
            step = at - starts[k]
            left_here = counts_ref[0, k] - step * LANES
            inside = jnp.logical_and(step >= 0, left_here > 0)
            tile = jnp.where(inside, k * per_segment + step, tile)
            left = jnp.where(inside, left_here, left)
        tile_at[t] = tile
        filled[t] = left
        return carry

    lax.fori_loop(0, chunks * width, list_tile, 0)

    rate = track_span / rows_grp / (2 * math.pi)
    start = lon_ref[0] * (1.0 / (2 * math.pi))
    for i in range(TILE_BLOCKS):
        mine = slice(i * LANES, (i + 1) * LANES)

        def down(row):
            return jnp.transpose(jnp.broadcast_to(index_ref[row:row + 1, mine], (LANES, LANES)).astype(jnp.float32))

        m = down(1)
        base = m * start - 0.25 * down(2)
        base = base - jnp.floor(base + 0.5)
        order[mine, :] = m
        first[mine, :] = base + m * (rate * lax.broadcasted_iota(jnp.int32, (LANES, LANES), 1).astype(jnp.float32))
    scale = 1.0 / math.sqrt(rows_grp * lax.axis_size("grp"))
    packed[...] = jnp.zeros_like(packed)

    def product(left, right):
        return lax.dot_general(left, right, (((1,), (1,)), ((), ())), preferred_element_type=jnp.float32)

    def add_chunk(c, carry):
        for j in range(len(peers)):
            chunk_copy(c, j).wait_recv()
        own_copy(c).wait()
        for i in range(width):
            t = c * width + i
            shift = tile_at[t].astype(jnp.float32) * (rate * LANES)
            count = filled[t]
            part_lanes = slice(i * LANES, (i + 1) * LANES)

            def wave_rows(r, carry):
                rows = pl.ds(pl.multiple_of(r * 64, 64), 64)
                values = got[c, pl.ds(r * (64 // cols), 64 // cols), :, part_lanes].reshape(64, LANES)
                turns = first[rows, :] + order[rows, :] * shift
                turns = turns - jnp.floor(turns + 0.5)
                g = 0.25 - jnp.abs(turns)
                z = g * g
                wave = jnp.full_like(z, SINE[-1] * scale)
                for term in SINE[-2::-1]:
                    wave = wave * z + term * scale
                lane = lax.broadcasted_iota(jnp.int32, (64, LANES), 1)
                values = jnp.where(lane < count, values * (wave * g), 0.0)
                upper = values.astype(jnp.bfloat16)
                high[rows, part_lanes] = upper
                low[rows, part_lanes] = (values - upper.astype(jnp.float32)).astype(jnp.bfloat16)
                return carry

            lax.fori_loop(0, total_cols // 64, wave_rows, 0)
        at = 0
        for i in range(TILE_BLOCKS):
            mine = slice(i * LANES, (i + 1) * LANES)
            rest = slice(i * LANES, total_cols)
            gram = product(high[mine, :], high[rest, :])
            gram += product(high[mine, :], low[rest, :])
            gram += product(low[mine, :], high[rest, :])
            for k in range(TILE_BLOCKS - i):
                packed[at * LANES:(at + 1) * LANES, :] += gram[:, k * LANES:(k + 1) * LANES]
                at += 1
        return carry

    lax.fori_loop(0, chunks, add_chunk, 0)

    sends = reduce_everywhere(me, depth, packed, other, part, plane, piece, total, *step_sems)
    out_ref[...] = total[...]
    for copy in sends:
        copy.wait_send()

    def drain(c, carry):
        for j in range(len(peers)):
            chunk_copy(c, j).wait_send()
        return carry

    lax.fori_loop(0, chunks, drain, 0)


def panel_gram(legendre, lon_center, counts, column_index):
    cols, rows_grp = legendre.shape
    segments = counts.shape[1]
    total_cols = column_index.shape[1]
    tiles = (rows_grp * 3 // 4) // LANES + segments
    width = 5
    chunks = -(-tiles // (segments * width))
    packed_rows = len(UPPER) * LANES
    share = packed_rows // segments
    peers, layers = len(OFFSETS), len(DEPTHS)
    f32 = jnp.float32
    dma = pltpu.SemaphoreType.DMA
    own = compact(legendre, counts, chunks * segments * width * LANES)
    return pl.pallas_call(
        lambda *refs: gram_kernel(rows_grp, width, *refs),
        out_shape=jax.ShapeDtypeStruct((packed_rows, LANES), f32),
        in_specs=[
            pl.BlockSpec(memory_space=pltpu.SMEM),
            pl.BlockSpec(memory_space=pltpu.SMEM),
            pl.BlockSpec(memory_space=pltpu.VMEM),
            pl.BlockSpec(memory_space=pl.ANY),
        ],
        out_specs=pl.BlockSpec(memory_space=pltpu.VMEM),
        scratch_shapes=[
            pltpu.SMEM((segments,), jnp.int32),
            pltpu.SMEM((chunks * width,), jnp.int32),
            pltpu.SMEM((chunks * width,), jnp.int32),
            pltpu.VMEM((total_cols, LANES), f32),
            pltpu.VMEM((total_cols, LANES), f32),
            pltpu.VMEM((chunks, segments, cols, width * LANES), f32),
            pltpu.VMEM((total_cols, width * LANES), jnp.bfloat16),
            pltpu.VMEM((total_cols, width * LANES), jnp.bfloat16),
            pltpu.VMEM((packed_rows, LANES), f32),
            pltpu.VMEM((packed_rows // 2, LANES), f32),
            pltpu.VMEM((len(CHIP_OFFSETS), share, LANES), f32),
            pltpu.VMEM((layers + 1, share, LANES), f32),
            pltpu.VMEM((share, LANES), f32),
            pltpu.VMEM((packed_rows, LANES), f32),
            dma((chunks,)),
            dma((chunks, peers)), dma((chunks, peers)),
            dma((len(SPANS),)), dma((len(SPANS),)),
            dma((len(SPANS), len(CHIP_OFFSETS))), dma((len(SPANS), len(CHIP_OFFSETS))),
            dma((len(SPANS), layers)), dma((len(SPANS), layers)),
            dma((len(SPANS), len(CHIP_OFFSETS))), dma((len(SPANS), len(CHIP_OFFSETS))),
            dma((len(SPANS), len(CHIP_OFFSETS) + 1)), dma((len(SPANS), len(CHIP_OFFSETS) + 1)),
        ],
        compiler_params=pltpu.CompilerParams(collective_id=0, has_side_effects=True, vmem_limit_bytes=24 * 2**20),
        name="panel_gram",
    )(lon_center, counts, column_index, own)


def lane_spread(v, j):
    return jnp.broadcast_to(v[:, j:j + 1], (8, 128))


def row_spread(v, i):
    return jnp.broadcast_to(v[i:i + 1, :], (8, 128))


def tree(terms):
    terms = list(terms)
    while len(terms) > 1:
        terms = [terms[i] + terms[i + 1] if i + 1 < len(terms) else terms[i] for i in range(0, len(terms), 2)]
    return terms[0]


def panel(a, out, k, p, tiles):
    base = 128 * k if isinstance(k, int) else pl.multiple_of(128 * k, 128)
    def cols(t):
        return pl.ds(base + 128 * t, 128)
    row = base + 8 * p
    sub = lax.broadcasted_iota(jnp.int32, (8, 128), 0)
    lane = lax.broadcasted_iota(jnp.int32, (8, 128), 1)
    rows = [a[pl.ds(row, 8), cols(t)] for t in range(tiles)]
    spread = [lane_spread(rows[0], 8 * p + j) for j in range(8)]
    e = {(i, j): row_spread(spread[j], i) for j in range(8) for i in range(j + 1)}
    m = {}
    n = {}
    for i in range(8):
        d = e[i, i]
        r = 1.0 / d
        s = lax.rsqrt(d)
        fac = {j: e[i, j] * r for j in range(i + 1, 8)}
        for j in range(i + 1, 8):
            for q in range(j, 8):
                e[j, q] = e[j, q] - fac[j] * e[i, q]
        for j in range(i + 1, 8):
            for c in range(i):
                m[j, c] = m[j, c] - fac[j] * m[i, c]
            m[j, i] = -fac[j]
        for c in range(i):
            n[i, c] = s * m[i, c]
        n[i, i] = s
    mcol = []
    for c in range(8):
        acc = jnp.zeros((8, 128), jnp.float32)
        for i in range(c, 8):
            acc = jnp.where(sub == i, n[i, c], acc)
        mcol.append(acc)
    pb = [[row_spread(rows[t], c) for c in range(8)] for t in range(tiles)]
    new = [tree(mcol[c] * pb[t][c] for c in range(8)) for t in range(tiles)]
    for t in range(tiles):
        val = new[t] if t else jnp.where(lane >= 8 * p + sub, new[0], 0.0)
        out[pl.ds(row, 8), cols(t)] = val
    if p == 15:
        return
    nb = [None] * tiles
    nb[0] = [tree(n[i, c] * pb[0][c] for c in range(i + 1)) for i in range(8)]
    for t in range(1, tiles):
        nb[t] = [row_spread(new[t], i) for i in range(8)]
    turned = jnp.transpose(new[0]) if p < 14 else None
    for q in range(p + 1, 16):
        grow = base + 8 * q
        g = [a[pl.ds(grow, 8), cols(t)] for t in range(tiles)]
        if q == p + 1:
            gc = [lane_spread(g[0], 8 * p + c) for c in range(8)]
            h = [tree(n[i, c] * gc[c] for c in range(i + 1)) for i in range(8)]
        else:
            tt = turned[8 * q:8 * q + 8, :]
            h = [jnp.broadcast_to(tt[:, i:i + 1], (8, 128)) for i in range(8)]
        for t in range(tiles):
            a[pl.ds(grow, 8), cols(t)] = g[t] - tree(h[i] * nb[t][i] for i in range(8))


def factor_kernel(index_ref, packed_ref, out, a):
    n = a.shape[0]
    out[...] = jnp.zeros((n, n), jnp.float32)
    degree = index_ref[0:1, :].astype(jnp.float32)
    kaula = kaula_gain * (degree / NMAX) ** 2
    diagonal = lax.broadcasted_iota(jnp.int32, (LANES, LANES), 0) == lax.broadcasted_iota(jnp.int32, (LANES, LANES), 1)
    for at, (i, j) in enumerate(UPPER):
        block = packed_ref[at * LANES:(at + 1) * LANES, :]
        if i == j:
            weight = kaula[:, i * LANES:(i + 1) * LANES]
            block = block + jnp.where(diagonal, weight * weight, 0.0)
        a[i * LANES:(i + 1) * LANES, j * LANES:(j + 1) * LANES] = block
    for k in range(TILE_BLOCKS):
        for p in range(16):
            panel(a, out, k, p, TILE_BLOCKS - k)
        done = slice(k * LANES, (k + 1) * LANES)
        for i in range(k + 1, TILE_BLOCKS):
            left = out[done, i * LANES:(i + 1) * LANES]
            a[i * LANES:(i + 1) * LANES, i * LANES:] -= lax.dot_general(
                left, out[done, i * LANES:], (((0,), (0,)), ((), ())), precision=highest,
                preferred_element_type=jnp.float32)


def upper_factor(packed, column_index):
    n = column_index.shape[1]
    return pl.pallas_call(
        factor_kernel,
        out_shape=jax.ShapeDtypeStruct((n, n), jnp.float32),
        in_specs=[pl.BlockSpec(memory_space=pltpu.VMEM)] * 2,
        out_specs=pl.BlockSpec(memory_space=pltpu.VMEM),
        scratch_shapes=[pltpu.VMEM((n, n), jnp.float32)],
        compiler_params=pltpu.CompilerParams(vmem_limit_bytes=16 * 2**20),
        name="upper_factor",
    )(column_index, packed)


def body(legendre, lon_center, counts, column_index):
    packed = panel_gram(legendre, lon_center, counts, column_index)
    return upper_factor(packed, column_index)


def solution(mesh):
    placed = (P("ord", "grp"), P("grp"), P("grp", None), P())
    return jax.shard_map(body, mesh=mesh, in_specs=placed, out_specs=P(), check_vma=False)
```

```python
import math

import jax
import jax.numpy as jnp
import numpy as np
from jax import lax
from jax.experimental import pallas as pl
from jax.experimental.pallas import tpu as pltpu
from jax.sharding import PartitionSpec as P

NMAX = 120

track_span = 0.3
kaula_gain = 1.2
highest = lax.Precision.HIGHEST
by_mesh = pl.DeviceIdType.MESH

LANES = 128
TILE_BLOCKS = 4
UPPER = [(i, j) for i in range(TILE_BLOCKS) for j in range(i, TILE_BLOCKS)]

CHIP_OFFSETS = [
    (2, 2), (2, 1), (1, 2), (2, 3), (3, 2), (2, 0), (0, 2), (1, 1), (3, 3), (1, 3), (3, 1),
    (1, 0), (0, 1), (3, 0), (0, 3),
]
OFFSETS = [(dx, dy, dc) for dc in (0, 1) for dx, dy in CHIP_OFFSETS] + [(0, 0, 1)]
DEPTHS = (4, 3, 5, 2, 6, 1, 7)
SPANS = (24, 16)


def sine_terms():
    g = np.cos(np.linspace(0.0, np.pi / 2, 400)) * 0.25
    g = g[g > 1e-4]
    powers = np.stack([g ** (2 * k + 1) for k in range(6)], axis=1)
    return [float(c) for c in np.linalg.lstsq(powers, np.sin(2 * np.pi * g), rcond=None)[0]]


SINE = sine_terms()


def remote(src, dst, sems, index, device):
    return pltpu.make_async_remote_copy(src_ref=src, dst_ref=dst, send_sem=sems[0].at[index], recv_sem=sems[1].at[index],
                                        device_id=device, device_id_type=by_mesh)


def reduce_everywhere(me, depth, packed, other, part, plane, piece, total, *sems):
    pair_sems, sems1, sems2, sems3, sems4 = [sems[2 * k:2 * k + 2] for k in range(5)]
    x, y, core = me // 8, (me // 2) % 4, me % 2
    partner = me + 1 - 2 * core
    chip = me // 2
    chips = [((x + dx) % 4) * 4 + (y + dy) % 4 for dx, dy in CHIP_OFFSETS]
    layers = [(depth + d) % 8 for d in DEPTHS]
    half_rows = other.shape[0]
    spans, at = [], 0
    for n in SPANS:
        spans.append((at, n))
        at += n
    def at_half(c, start, n):
        return pl.ds(pl.multiple_of(c * half_rows + start, 8), n)
    pair = []
    for s, (a, n) in enumerate(spans):
        pair.append(remote(packed.at[at_half(1 - core, a * 16, n * 16)], other.at[pl.ds(a * 16, n * 16)], pair_sems, s, {"ord": partner}))
    for copy in pair:
        copy.start()
    def rows(c, a, n):
        return a * 16 + c * n
    first, second, third, fourth = [], [], [], []
    for s, (a, n) in enumerate(spans):
        pair[s].wait_recv()
        mine = at_half(core, a * 16, n * 16)
        packed[mine, :] = packed[mine, :] + other[pl.ds(a * 16, n * 16), :]
        step = [remote(packed.at[at_half(core, rows(c, a, n), n)], part.at[j, pl.ds(a, n)], sems1, (s, j), {"ord": c * 2 + core}) for j, c in enumerate(chips)]
        for copy in step:
            copy.start()
        first.append(step)
    for s, (a, n) in enumerate(spans):
        value = packed[at_half(core, rows(chip, a, n), n), :]
        for j, copy in enumerate(first[s]):
            copy.wait_recv()
            value = value + part[j, pl.ds(a, n), :]
        plane[depth, pl.ds(a, n), :] = value
        step = [remote(plane.at[depth, pl.ds(a, n)], plane.at[depth, pl.ds(a, n)], sems2, (s, j), {"grp": l}) for j, l in enumerate(layers)]
        for copy in step:
            copy.start()
        second.append(step)
    for s, (a, n) in enumerate(spans):
        for copy in second[s]:
            copy.wait_recv()
        value = plane[0, pl.ds(a, n), :]
        for d in range(1, 8):
            value = value + plane[d, pl.ds(a, n), :]
        piece[pl.ds(a, n), :] = value
        home = at_half(core, rows(chip, a, n), n)
        step = [remote(piece.at[pl.ds(a, n)], total.at[home], sems3, (s, j), {"ord": c * 2 + core}) for j, c in enumerate(chips)]
        for copy in step:
            copy.start()
        third.append(step)
        keep = remote(piece.at[pl.ds(a, n)], total.at[home], sems4, (s, 15), {"ord": partner})
        keep.start()
        fourth.append([keep])
        total[home, :] = value
    back = [((x - dx) % 4) * 4 + (y - dy) % 4 for dx, dy in CHIP_OFFSETS]
    for s, (a, n) in enumerate(spans):
        for j in reversed(range(15)):
            third[s][j].wait_recv()
            spot = total.at[at_half(core, rows(back[j], a, n), n)]
            copy = remote(spot, spot, sems4, (s, j), {"ord": partner})
            copy.start()
            fourth[s].append(copy)
    for s in range(len(spans)):
        for copy in fourth[s]:
            copy.wait_recv()
    return pair + [c for group in first + second + third + fourth for c in group]


def tiles_in(count):
    return lax.shift_right_logical(count + (LANES - 1), 7)


def compact_kernel(counts_ref, legendre_ref, out_ref, sem):
    segments = counts_ref.shape[1]
    per_segment = legendre_ref.shape[1] // segments // LANES
    sizes = [1 << b for b in reversed(range(per_segment.bit_length()))]

    def span(at, size):
        return pl.ds(pl.multiple_of(at * LANES, LANES), size * LANES)

    def segment(k, to):
        n = tiles_in(counts_ref[0, k])
        at = k * per_segment
        for size in sizes:
            has = (n & size) != 0

            @pl.when(has)
            def _(at=at, to=to, size=size):
                pltpu.make_async_copy(legendre_ref.at[:, span(at, size)], out_ref.at[:, span(to, size)], sem).start()

            step = jnp.where(has, size, 0)
            at, to = at + step, to + step
        return to

    moved = lax.fori_loop(0, segments, segment, jnp.int32(0))
    for b in reversed(range((out_ref.shape[1] // LANES).bit_length())):
        @pl.when((moved & (1 << b)) != 0)
        def _(b=b):
            whole = pl.ds(0, LANES << b)
            pltpu.make_async_copy(legendre_ref.at[:, whole], out_ref.at[:, whole], sem).wait()


def compact(legendre, counts, lanes):
    return pl.pallas_call(
        compact_kernel,
        out_shape=jax.ShapeDtypeStruct((legendre.shape[0], lanes), jnp.float32),
        in_specs=[pl.BlockSpec(memory_space=pltpu.SMEM), pl.BlockSpec(memory_space=pltpu.HBM)],
        out_specs=pl.BlockSpec(memory_space=pltpu.VMEM),
        scratch_shapes=[pltpu.SemaphoreType.DMA],
        compiler_params=pltpu.CompilerParams(vmem_limit_bytes=44 * 2**20),
        name="compact",
    )(counts, legendre)


def gram_kernel(rows_grp, width, lon_ref, counts_ref, index_ref, own_ref, out_ref,
                starts, tile_at, filled, order, first, got, high, low, packed, other, part, plane, piece, total,
                own_sem, send_sem, recv_sem, *step_sems):
    me = lax.axis_index("ord")
    depth = lax.axis_index("grp")
    segments = counts_ref.shape[1]
    per_segment = rows_grp // segments // LANES
    chunks, _, cols, lanes = got.shape
    total_cols = segments * cols
    x, y, core = me // 8, (me // 2) % 4, me % 2

    def neighbour(offset):
        dx, dy, dc = offset
        return ((x + dx) % 4) * 8 + ((y + dy) % 4) * 2 + (core + dc) % 2

    peers = [neighbour(o) for o in OFFSETS]
    layers = [(depth + d) % 8 for d in DEPTHS]

    barrier = pltpu.get_barrier_semaphore()
    for peer in peers:
        pl.semaphore_signal(barrier, inc=1, device_id={"ord": peer}, device_id_type=by_mesh)
    for layer in layers:
        pl.semaphore_signal(barrier, inc=1, device_id={"grp": layer}, device_id_type=by_mesh)
    pl.semaphore_wait(barrier, len(peers) + len(layers))

    def own_tiles(c, d):
        return own_ref.at[:, pl.ds(pl.multiple_of((c * segments + d) * lanes, LANES), lanes)]

    def chunk_copy(c, j):
        return pltpu.make_async_remote_copy(
            src_ref=own_tiles(c, peers[j]), dst_ref=got.at[c, me], send_sem=send_sem.at[c, j],
            recv_sem=recv_sem.at[c, j], device_id={"ord": peers[j]}, device_id_type=by_mesh)

    def own_copy(c):
        return pltpu.make_async_copy(own_tiles(c, me), got.at[c, me], own_sem.at[c])

    def send_chunk(c, carry):
        for j in range(len(peers)):
            chunk_copy(c, j).start()
        own_copy(c).start()
        return carry

    lax.fori_loop(0, chunks, send_chunk, 0)

    begin = jnp.int32(0)
    for k in range(segments):
        starts[k] = begin
        begin = begin + tiles_in(counts_ref[0, k])

    def list_tile(t, carry):
        at = (t // width * segments + me) * width + t % width
        tile, left = jnp.int32(0), jnp.int32(0)
        for k in range(segments):
            step = at - starts[k]
            left_here = counts_ref[0, k] - step * LANES
            inside = jnp.logical_and(step >= 0, left_here > 0)
            tile = jnp.where(inside, k * per_segment + step, tile)
            left = jnp.where(inside, left_here, left)
        tile_at[t] = tile
        filled[t] = left
        return carry

    lax.fori_loop(0, chunks * width, list_tile, 0)

    rate = track_span / rows_grp / (2 * math.pi)
    start = lon_ref[0] * (1.0 / (2 * math.pi))
    for i in range(TILE_BLOCKS):
        mine = slice(i * LANES, (i + 1) * LANES)

        def down(row):
            return jnp.transpose(jnp.broadcast_to(index_ref[row:row + 1, mine], (LANES, LANES)).astype(jnp.float32))

        m = down(1)
        base = m * start - 0.25 * down(2)
        base = base - jnp.floor(base + 0.5)
        order[mine, :] = m
        first[mine, :] = base + m * (rate * lax.broadcasted_iota(jnp.int32, (LANES, LANES), 1).astype(jnp.float32))
    scale = 1.0 / math.sqrt(rows_grp * lax.axis_size("grp"))
    packed[...] = jnp.zeros_like(packed)

    def product(left, right):
        return lax.dot_general(left, right, (((1,), (1,)), ((), ())), preferred_element_type=jnp.float32)

    def add_chunk(c, carry):
        for j in range(len(peers)):
            chunk_copy(c, j).wait_recv()
        own_copy(c).wait()
        for i in range(width):
            t = c * width + i
            shift = tile_at[t].astype(jnp.float32) * (rate * LANES)
            count = filled[t]
            part_lanes = slice(i * LANES, (i + 1) * LANES)

            def wave_rows(r, carry):
                rows = pl.ds(pl.multiple_of(r * 64, 64), 64)
                values = got[c, pl.ds(r * (64 // cols), 64 // cols), :, part_lanes].reshape(64, LANES)
                turns = first[rows, :] + order[rows, :] * shift
                turns = turns - jnp.floor(turns + 0.5)
                g = 0.25 - jnp.abs(turns)
                z = g * g
                wave = jnp.full_like(z, SINE[-1] * scale)
                for term in SINE[-2::-1]:
                    wave = wave * z + term * scale
                lane = lax.broadcasted_iota(jnp.int32, (64, LANES), 1)
                values = jnp.where(lane < count, values * (wave * g), 0.0)
                upper = values.astype(jnp.bfloat16)
                high[rows, part_lanes] = upper
                low[rows, part_lanes] = (values - upper.astype(jnp.float32)).astype(jnp.bfloat16)
                return carry

            lax.fori_loop(0, total_cols // 64, wave_rows, 0)
        at = 0
        for i in range(TILE_BLOCKS):
            mine = slice(i * LANES, (i + 1) * LANES)
            rest = slice(i * LANES, total_cols)
            gram = product(high[mine, :], high[rest, :])
            gram += product(high[mine, :], low[rest, :])
            gram += product(low[mine, :], high[rest, :])
            for k in range(TILE_BLOCKS - i):
                packed[at * LANES:(at + 1) * LANES, :] += gram[:, k * LANES:(k + 1) * LANES]
                at += 1
        return carry

    lax.fori_loop(0, chunks, add_chunk, 0)

    sends = reduce_everywhere(me, depth, packed, other, part, plane, piece, total, *step_sems)
    out_ref[...] = total[...]
    for copy in sends:
        copy.wait_send()

    def drain(c, carry):
        for j in range(len(peers)):
            chunk_copy(c, j).wait_send()
        return carry

    lax.fori_loop(0, chunks, drain, 0)


def panel_gram(legendre, lon_center, counts, column_index):
    cols, rows_grp = legendre.shape
    segments = counts.shape[1]
    total_cols = column_index.shape[1]
    tiles = (rows_grp * 3 // 4) // LANES + segments
    width = 5
    chunks = -(-tiles // (segments * width))
    packed_rows = len(UPPER) * LANES
    share = packed_rows // segments
    peers, layers = len(OFFSETS), len(DEPTHS)
    f32 = jnp.float32
    dma = pltpu.SemaphoreType.DMA
    own = compact(legendre, counts, chunks * segments * width * LANES)
    return pl.pallas_call(
        lambda *refs: gram_kernel(rows_grp, width, *refs),
        out_shape=jax.ShapeDtypeStruct((packed_rows, LANES), f32),
        in_specs=[
            pl.BlockSpec(memory_space=pltpu.SMEM),
            pl.BlockSpec(memory_space=pltpu.SMEM),
            pl.BlockSpec(memory_space=pltpu.VMEM),
            pl.BlockSpec(memory_space=pl.ANY),
        ],
        out_specs=pl.BlockSpec(memory_space=pltpu.VMEM),
        scratch_shapes=[
            pltpu.SMEM((segments,), jnp.int32),
            pltpu.SMEM((chunks * width,), jnp.int32),
            pltpu.SMEM((chunks * width,), jnp.int32),
            pltpu.VMEM((total_cols, LANES), f32),
            pltpu.VMEM((total_cols, LANES), f32),
            pltpu.VMEM((chunks, segments, cols, width * LANES), f32),
            pltpu.VMEM((total_cols, width * LANES), jnp.bfloat16),
            pltpu.VMEM((total_cols, width * LANES), jnp.bfloat16),
            pltpu.VMEM((packed_rows, LANES), f32),
            pltpu.VMEM((packed_rows // 2, LANES), f32),
            pltpu.VMEM((len(CHIP_OFFSETS), share, LANES), f32),
            pltpu.VMEM((layers + 1, share, LANES), f32),
            pltpu.VMEM((share, LANES), f32),
            pltpu.VMEM((packed_rows, LANES), f32),
            dma((chunks,)),
            dma((chunks, peers)), dma((chunks, peers)),
            dma((len(SPANS),)), dma((len(SPANS),)),
            dma((len(SPANS), len(CHIP_OFFSETS))), dma((len(SPANS), len(CHIP_OFFSETS))),
            dma((len(SPANS), layers)), dma((len(SPANS), layers)),
            dma((len(SPANS), len(CHIP_OFFSETS))), dma((len(SPANS), len(CHIP_OFFSETS))),
            dma((len(SPANS), len(CHIP_OFFSETS) + 1)), dma((len(SPANS), len(CHIP_OFFSETS) + 1)),
        ],
        compiler_params=pltpu.CompilerParams(collective_id=0, has_side_effects=True, vmem_limit_bytes=24 * 2**20),
        name="panel_gram",
    )(lon_center, counts, column_index, own)


def lane_spread(v, j):
    return jnp.broadcast_to(v[:, j:j + 1], (8, 128))


def row_spread(v, i):
    return jnp.broadcast_to(v[i:i + 1, :], (8, 128))


def tree(terms):
    terms = list(terms)
    while len(terms) > 1:
        terms = [terms[i] + terms[i + 1] if i + 1 < len(terms) else terms[i] for i in range(0, len(terms), 2)]
    return terms[0]


def panel(a, out, k, p, tiles, spread):
    base = 128 * k
    row = base + 8 * p
    sub = lax.broadcasted_iota(jnp.int32, (8, 128), 0)
    lane = lax.broadcasted_iota(jnp.int32, (8, 128), 1)

    def load(q):
        return [a[base + 8 * q:base + 8 * q + 8, base + 128 * t:base + 128 * t + 128] for t in range(tiles)]

    rows = load(p)
    if p == 0:
        spread = [lane_spread(rows[0], j) for j in range(8)]
    spread = list(spread)
    near = range(p + 1, min(p + 4, 16))
    groups = {q: load(q) for q in near}
    columns = {q: [lane_spread(groups[q][0], 8 * p + c) for c in range(8)] for q in near}
    done = [[] for _ in range(tiles)]
    for i in range(8):
        s = lax.rsqrt(row_spread(spread[i], i))
        u = spread[i] * s
        for q in near:
            columns[q][i] = columns[q][i] * s
        for j in range(i + 1, 8):
            f = row_spread(u, j)
            spread[j] = spread[j] - u * f
            for q in near:
                columns[q][j] = columns[q][j] - f * columns[q][i]
        for t in range(tiles):
            final = row_spread(rows[t], i) * s
            done[t].append(final)
            if i < 7:
                rows[t] = rows[t] - u * final
    for t in range(tiles):
        val = done[t][0]
        for i in range(1, 8):
            val = jnp.where(sub == i, done[t][i], val)
        if t == 0:
            new = val
            val = jnp.where(lane >= 8 * p + sub, val, 0.0)
        out[row:row + 8, base + 128 * t:base + 128 * t + 128] = val
    if p == 15:
        return None
    first = columns[p + 1]
    ahead = []
    for c in range(8):
        total = tree(first[i] * row_spread(first[i], c) for i in range(8))
        ahead.append(lane_spread(groups[p + 1][0], 8 * (p + 1) + c) - total)
    turned = jnp.transpose(new) if p < 12 else None
    for q in range(p + 1, 16):
        if q in near:
            g, h = groups[q], columns[q]
        else:
            g = load(q)
            h = [jnp.broadcast_to(turned[8 * q:8 * q + 8, i:i + 1], (8, 128)) for i in range(8)]
        for t in range(tiles):
            a[base + 8 * q:base + 8 * q + 8, base + 128 * t:base + 128 * t + 128] = g[t] - tree(h[i] * done[t][i] for i in range(8))
    return ahead


def factor_kernel(index_ref, packed_ref, out, a):
    n = a.shape[0]
    out[...] = jnp.zeros((n, n), jnp.float32)
    degree = index_ref[0:1, :].astype(jnp.float32)
    kaula = kaula_gain * (degree / NMAX) ** 2
    diagonal = lax.broadcasted_iota(jnp.int32, (LANES, LANES), 0) == lax.broadcasted_iota(jnp.int32, (LANES, LANES), 1)
    for at, (i, j) in enumerate(UPPER):
        block = packed_ref[at * LANES:(at + 1) * LANES, :]
        if i == j:
            weight = kaula[:, i * LANES:(i + 1) * LANES]
            block = block + jnp.where(diagonal, weight * weight, 0.0)
        a[i * LANES:(i + 1) * LANES, j * LANES:(j + 1) * LANES] = block
    for k in range(TILE_BLOCKS):
        ahead = None
        for p in range(16):
            ahead = panel(a, out, k, p, TILE_BLOCKS - k, ahead)
        done = slice(k * LANES, (k + 1) * LANES)
        for i in range(k + 1, TILE_BLOCKS):
            left = out[done, i * LANES:(i + 1) * LANES]
            a[i * LANES:(i + 1) * LANES, i * LANES:] -= lax.dot_general(
                left, out[done, i * LANES:], (((0,), (0,)), ((), ())), precision=highest,
                preferred_element_type=jnp.float32)


def upper_factor(packed, column_index):
    n = column_index.shape[1]
    return pl.pallas_call(
        factor_kernel,
        out_shape=jax.ShapeDtypeStruct((n, n), jnp.float32),
        in_specs=[pl.BlockSpec(memory_space=pltpu.VMEM)] * 2,
        out_specs=pl.BlockSpec(memory_space=pltpu.VMEM),
        scratch_shapes=[pltpu.VMEM((n, n), jnp.float32)],
        compiler_params=pltpu.CompilerParams(vmem_limit_bytes=16 * 2**20),
        name="upper_factor",
    )(column_index, packed)


def body(legendre, lon_center, counts, column_index):
    packed = panel_gram(legendre, lon_center, counts, column_index)
    return upper_factor(packed, column_index)


def solution(mesh):
    placed = (P("ord", "grp"), P("grp"), P("grp", None), P())
    return jax.shard_map(body, mesh=mesh, in_specs=placed, out_specs=P(), check_vma=False)
```

```python
import math

import jax
import jax.numpy as jnp
import numpy as np
from jax import lax
from jax.experimental import pallas as pl
from jax.experimental.pallas import tpu as pltpu
from jax.sharding import PartitionSpec as P

NMAX = 120

track_span = 0.3
kaula_gain = 1.2
highest = lax.Precision.HIGHEST
by_mesh = pl.DeviceIdType.MESH

LANES = 128
TILE_BLOCKS = 4
UPPER = [(i, j) for i in range(TILE_BLOCKS) for j in range(i, TILE_BLOCKS)]

CHIP_OFFSETS = [
    (2, 2), (2, 1), (1, 2), (2, 3), (3, 2), (2, 0), (0, 2), (1, 1), (3, 3), (1, 3), (3, 1),
    (1, 0), (0, 1), (3, 0), (0, 3),
]
OFFSETS = [(dx, dy, dc) for dc in (0, 1) for dx, dy in CHIP_OFFSETS] + [(0, 0, 1)]
DEPTHS = (4, 3, 5, 2, 6, 1, 7)
SPANS = (24, 16)


def sine_terms():
    g = np.cos(np.linspace(0.0, np.pi / 2, 400)) * 0.25
    g = g[g > 1e-4]
    powers = np.stack([g ** (2 * k + 1) for k in range(6)], axis=1)
    return [float(c) for c in np.linalg.lstsq(powers, np.sin(2 * np.pi * g), rcond=None)[0]]


SINE = sine_terms()


def remote(src, dst, sems, index, device):
    return pltpu.make_async_remote_copy(src_ref=src, dst_ref=dst, send_sem=sems[0].at[index], recv_sem=sems[1].at[index],
                                        device_id=device, device_id_type=by_mesh)


def reduce_everywhere(me, depth, packed, other, part, plane, piece, total, *sems):
    pair_sems, sems1, sems2, sems3, sems4 = [sems[2 * k:2 * k + 2] for k in range(5)]
    x, y, core = me // 8, (me // 2) % 4, me % 2
    partner = me + 1 - 2 * core
    chip = me // 2
    chips = [((x + dx) % 4) * 4 + (y + dy) % 4 for dx, dy in CHIP_OFFSETS]
    layers = [(depth + d) % 8 for d in DEPTHS]
    half_rows = other.shape[0]
    spans, at = [], 0
    for n in SPANS:
        spans.append((at, n))
        at += n
    def at_half(c, start, n):
        return pl.ds(pl.multiple_of(c * half_rows + start, 8), n)
    pair = []
    for s, (a, n) in enumerate(spans):
        pair.append(remote(packed.at[at_half(1 - core, a * 16, n * 16)], other.at[pl.ds(a * 16, n * 16)], pair_sems, s, {"ord": partner}))
    for copy in pair:
        copy.start()
    def rows(c, a, n):
        return a * 16 + c * n
    first, second, third, fourth = [], [], [], []
    for s, (a, n) in enumerate(spans):
        pair[s].wait_recv()
        mine = at_half(core, a * 16, n * 16)
        packed[mine, :] = packed[mine, :] + other[pl.ds(a * 16, n * 16), :]
        step = [remote(packed.at[at_half(core, rows(c, a, n), n)], part.at[j, pl.ds(a, n)], sems1, (s, j), {"ord": c * 2 + core}) for j, c in enumerate(chips)]
        for copy in step:
            copy.start()
        first.append(step)
    for s, (a, n) in enumerate(spans):
        value = packed[at_half(core, rows(chip, a, n), n), :]
        for j, copy in enumerate(first[s]):
            copy.wait_recv()
            value = value + part[j, pl.ds(a, n), :]
        plane[depth, pl.ds(a, n), :] = value
        step = [remote(plane.at[depth, pl.ds(a, n)], plane.at[depth, pl.ds(a, n)], sems2, (s, j), {"grp": l}) for j, l in enumerate(layers)]
        for copy in step:
            copy.start()
        second.append(step)
    for s, (a, n) in enumerate(spans):
        for copy in second[s]:
            copy.wait_recv()
        value = plane[0, pl.ds(a, n), :]
        for d in range(1, 8):
            value = value + plane[d, pl.ds(a, n), :]
        piece[pl.ds(a, n), :] = value
        home = at_half(core, rows(chip, a, n), n)
        step = [remote(piece.at[pl.ds(a, n)], total.at[home], sems3, (s, j), {"ord": c * 2 + core}) for j, c in enumerate(chips)]
        for copy in step:
            copy.start()
        third.append(step)
        keep = remote(piece.at[pl.ds(a, n)], total.at[home], sems4, (s, 15), {"ord": partner})
        keep.start()
        fourth.append([keep])
        total[home, :] = value
    back = [((x - dx) % 4) * 4 + (y - dy) % 4 for dx, dy in CHIP_OFFSETS]
    for s, (a, n) in enumerate(spans):
        for j in reversed(range(15)):
            third[s][j].wait_recv()
            spot = total.at[at_half(core, rows(back[j], a, n), n)]
            copy = remote(spot, spot, sems4, (s, j), {"ord": partner})
            copy.start()
            fourth[s].append(copy)
    for s in range(len(spans)):
        for copy in fourth[s]:
            copy.wait_recv()
    return pair + [c for group in first + second + third + fourth for c in group]


def tiles_in(count):
    return lax.shift_right_logical(count + (LANES - 1), 7)


def compact_kernel(counts_ref, legendre_ref, out_ref, sem):
    segments = counts_ref.shape[1]
    per_segment = legendre_ref.shape[1] // segments // LANES
    sizes = [1 << b for b in reversed(range(per_segment.bit_length()))]

    def span(at, size):
        return pl.ds(pl.multiple_of(at * LANES, LANES), size * LANES)

    def segment(k, to):
        n = tiles_in(counts_ref[0, k])
        at = k * per_segment
        for size in sizes:
            has = (n & size) != 0

            @pl.when(has)
            def _(at=at, to=to, size=size):
                pltpu.make_async_copy(legendre_ref.at[:, span(at, size)], out_ref.at[:, span(to, size)], sem).start()

            step = jnp.where(has, size, 0)
            at, to = at + step, to + step
        return to

    moved = lax.fori_loop(0, segments, segment, jnp.int32(0))
    for b in reversed(range((out_ref.shape[1] // LANES).bit_length())):
        @pl.when((moved & (1 << b)) != 0)
        def _(b=b):
            whole = pl.ds(0, LANES << b)
            pltpu.make_async_copy(legendre_ref.at[:, whole], out_ref.at[:, whole], sem).wait()


def compact(legendre, counts, lanes):
    return pl.pallas_call(
        compact_kernel,
        out_shape=jax.ShapeDtypeStruct((legendre.shape[0], lanes), jnp.float32),
        in_specs=[pl.BlockSpec(memory_space=pltpu.SMEM), pl.BlockSpec(memory_space=pltpu.HBM)],
        out_specs=pl.BlockSpec(memory_space=pltpu.VMEM),
        scratch_shapes=[pltpu.SemaphoreType.DMA],
        compiler_params=pltpu.CompilerParams(vmem_limit_bytes=44 * 2**20),
        name="compact",
    )(counts, legendre)


def gram_kernel(rows_grp, lon_ref, counts_ref, index_ref, own_ref, out_ref,
                starts, tile_at, filled, order, first, got, got_last, high, low, packed, other, part, plane, piece, total,
                own_sem, send_sem, recv_sem, *step_sems):
    me = lax.axis_index("ord")
    depth = lax.axis_index("grp")
    segments = counts_ref.shape[1]
    per_segment = rows_grp // segments // LANES
    chunks, _, cols, lanes = got.shape
    width = lanes // LANES
    total_cols = segments * cols
    x, y, core = me // 8, (me // 2) % 4, me % 2

    def neighbour(offset):
        dx, dy, dc = offset
        dx, dy = dx + core * (dy - dx), dy + core * (dx - dy)
        return ((x + dx) % 4) * 8 + ((y + dy) % 4) * 2 + (core + dc) % 2

    peers = [neighbour(o) for o in OFFSETS]
    layers = [(depth + d) % 8 for d in DEPTHS]

    barrier = pltpu.get_barrier_semaphore()
    for peer in peers:
        pl.semaphore_signal(barrier, inc=1, device_id={"ord": peer}, device_id_type=by_mesh)
    for layer in layers:
        pl.semaphore_signal(barrier, inc=1, device_id={"grp": layer}, device_id_type=by_mesh)
    pl.semaphore_wait(barrier, len(peers) + len(layers))

    def own_tiles(c, d):
        return own_ref.at[:, pl.ds(pl.multiple_of((c * segments + d) * lanes, LANES), lanes)]

    def last_tile(d):
        return own_ref.at[:, pl.ds(pl.multiple_of(chunks * segments * lanes + d * LANES, LANES), LANES)]

    def send(src, dst, c, j):
        return pltpu.make_async_remote_copy(
            src_ref=src, dst_ref=dst, send_sem=send_sem.at[c, j], recv_sem=recv_sem.at[c, j],
            device_id={"ord": peers[j]}, device_id_type=by_mesh)

    def chunk_copies(c):
        return [send(own_tiles(c, peers[j]), got.at[c, me], c, j) for j in range(len(peers))]

    last_copies = [send(last_tile(peers[j]), got_last.at[me], chunks, j) for j in range(len(peers))]

    def own_copy(c):
        return pltpu.make_async_copy(own_tiles(c, me), got.at[c, me], own_sem.at[c])

    own_last = pltpu.make_async_copy(last_tile(me), got_last.at[me], own_sem.at[chunks])

    def send_chunk(c, carry):
        for copy in chunk_copies(c):
            copy.start()
        own_copy(c).start()
        return carry

    lax.fori_loop(0, chunks, send_chunk, 0)
    for copy in last_copies:
        copy.start()
    own_last.start()

    begin = jnp.int32(0)
    for k in range(segments):
        starts[k] = begin
        begin = begin + tiles_in(counts_ref[0, k])

    def list_tile(t, carry):
        at = (t // width * segments + me) * width + t % width
        at = jnp.where(t < chunks * width, at, chunks * segments * width + me)
        tile, left = jnp.int32(0), jnp.int32(0)
        for k in range(segments):
            step = at - starts[k]
            left_here = counts_ref[0, k] - step * LANES
            inside = jnp.logical_and(step >= 0, left_here > 0)
            tile = jnp.where(inside, k * per_segment + step, tile)
            left = jnp.where(inside, left_here, left)
        tile_at[t] = tile
        filled[t] = left
        return carry

    lax.fori_loop(0, chunks * width + 1, list_tile, 0)

    rate = track_span / rows_grp / (2 * math.pi)
    start = lon_ref[0] * (1.0 / (2 * math.pi))
    for i in range(TILE_BLOCKS):
        mine = slice(i * LANES, (i + 1) * LANES)

        def down(row):
            return jnp.transpose(jnp.broadcast_to(index_ref[row:row + 1, mine], (LANES, LANES)).astype(jnp.float32))

        m = down(1)
        base = m * start - 0.25 * down(2)
        base = base - jnp.floor(base + 0.5)
        order[mine, :] = m
        first[mine, :] = base + m * (rate * lax.broadcasted_iota(jnp.int32, (LANES, LANES), 1).astype(jnp.float32))
    scale = 1.0 / math.sqrt(rows_grp * lax.axis_size("grp"))
    packed[...] = jnp.zeros_like(packed)

    def product(left, right):
        return lax.dot_general(left, right, (((1,), (1,)), ((), ())), preferred_element_type=jnp.float32)

    def add_tiles(tiles_ref, first_tile, count_tiles):
        for i in range(count_tiles):
            t = first_tile + i
            shift = tile_at[t].astype(jnp.float32) * (rate * LANES)
            count = filled[t]
            part_lanes = slice(i * LANES, (i + 1) * LANES)

            def wave_rows(r, carry):
                rows = pl.ds(pl.multiple_of(r * 64, 64), 64)
                values = tiles_ref[pl.ds(r * (64 // cols), 64 // cols), :, part_lanes].reshape(64, LANES)
                turns = first[rows, :] + order[rows, :] * shift
                turns = turns - jnp.floor(turns + 0.5)
                g = 0.25 - jnp.abs(turns)
                z = g * g
                wave = jnp.full_like(z, SINE[-1] * scale)
                for term in SINE[-2::-1]:
                    wave = wave * z + term * scale
                lane = lax.broadcasted_iota(jnp.int32, (64, LANES), 1)
                values = jnp.where(lane < count, values * (wave * g), 0.0)
                upper = values.astype(jnp.bfloat16)
                high[rows, part_lanes] = upper
                low[rows, part_lanes] = (values - upper.astype(jnp.float32)).astype(jnp.bfloat16)
                return carry

            lax.fori_loop(0, total_cols // 64, wave_rows, 0)
        depth_lanes = slice(0, count_tiles * LANES)
        at = 0
        for i in range(TILE_BLOCKS):
            mine = slice(i * LANES, (i + 1) * LANES)
            rest = slice(i * LANES, total_cols)
            gram = product(high[mine, depth_lanes], high[rest, depth_lanes])
            gram += product(high[mine, depth_lanes], low[rest, depth_lanes])
            gram += product(low[mine, depth_lanes], high[rest, depth_lanes])
            for k in range(TILE_BLOCKS - i):
                packed[at * LANES:(at + 1) * LANES, :] += gram[:, k * LANES:(k + 1) * LANES]
                at += 1

    def add_chunk(c, carry):
        for copy in chunk_copies(c):
            copy.wait_recv()
        own_copy(c).wait()
        add_tiles(got.at[c], c * width, width)
        return carry

    lax.fori_loop(0, chunks, add_chunk, 0)
    for copy in last_copies:
        copy.wait_recv()
    own_last.wait()
    add_tiles(got_last, chunks * width, 1)

    sends = reduce_everywhere(me, depth, packed, other, part, plane, piece, total, *step_sems)
    out_ref[...] = total[...]
    for copy in sends:
        copy.wait_send()

    def drain(c, carry):
        for copy in chunk_copies(c):
            copy.wait_send()
        return carry

    lax.fori_loop(0, chunks, drain, 0)
    for copy in last_copies:
        copy.wait_send()


def panel_gram(legendre, lon_center, counts, column_index):
    cols, rows_grp = legendre.shape
    segments = counts.shape[1]
    total_cols = column_index.shape[1]
    tiles = (rows_grp * 3 // 4) // LANES + segments
    per_device = -(-tiles // segments)
    width = 6
    chunks = (per_device - 1) // width
    assert chunks * width + 1 == per_device
    packed_rows = len(UPPER) * LANES
    share = packed_rows // segments
    peers, layers = len(OFFSETS), len(DEPTHS)
    f32 = jnp.float32
    dma = pltpu.SemaphoreType.DMA
    own = compact(legendre, counts, segments * per_device * LANES)
    return pl.pallas_call(
        lambda *refs: gram_kernel(rows_grp, *refs),
        out_shape=jax.ShapeDtypeStruct((packed_rows, LANES), f32),
        in_specs=[
            pl.BlockSpec(memory_space=pltpu.SMEM),
            pl.BlockSpec(memory_space=pltpu.SMEM),
            pl.BlockSpec(memory_space=pltpu.VMEM),
            pl.BlockSpec(memory_space=pl.ANY),
        ],
        out_specs=pl.BlockSpec(memory_space=pltpu.VMEM),
        scratch_shapes=[
            pltpu.SMEM((segments,), jnp.int32),
            pltpu.SMEM((per_device,), jnp.int32),
            pltpu.SMEM((per_device,), jnp.int32),
            pltpu.VMEM((total_cols, LANES), f32),
            pltpu.VMEM((total_cols, LANES), f32),
            pltpu.VMEM((chunks, segments, cols, width * LANES), f32),
            pltpu.VMEM((segments, cols, LANES), f32),
            pltpu.VMEM((total_cols, width * LANES), jnp.bfloat16),
            pltpu.VMEM((total_cols, width * LANES), jnp.bfloat16),
            pltpu.VMEM((packed_rows, LANES), f32),
            pltpu.VMEM((packed_rows // 2, LANES), f32),
            pltpu.VMEM((len(CHIP_OFFSETS), share, LANES), f32),
            pltpu.VMEM((layers + 1, share, LANES), f32),
            pltpu.VMEM((share, LANES), f32),
            pltpu.VMEM((packed_rows, LANES), f32),
            dma((chunks + 1,)),
            dma((chunks + 1, peers)), dma((chunks + 1, peers)),
            dma((len(SPANS),)), dma((len(SPANS),)),
            dma((len(SPANS), len(CHIP_OFFSETS))), dma((len(SPANS), len(CHIP_OFFSETS))),
            dma((len(SPANS), layers)), dma((len(SPANS), layers)),
            dma((len(SPANS), len(CHIP_OFFSETS))), dma((len(SPANS), len(CHIP_OFFSETS))),
            dma((len(SPANS), len(CHIP_OFFSETS) + 1)), dma((len(SPANS), len(CHIP_OFFSETS) + 1)),
        ],
        compiler_params=pltpu.CompilerParams(collective_id=0, has_side_effects=True, vmem_limit_bytes=24 * 2**20),
        name="panel_gram",
    )(lon_center, counts, column_index, own)


def lane_spread(v, j):
    return jnp.broadcast_to(v[:, j:j + 1], (8, 128))


def row_spread(v, i):
    return jnp.broadcast_to(v[i:i + 1, :], (8, 128))


def tree(terms):
    terms = list(terms)
    while len(terms) > 1:
        terms = [terms[i] + terms[i + 1] if i + 1 < len(terms) else terms[i] for i in range(0, len(terms), 2)]
    return terms[0]


def panel(a, out, k, p, tiles, spread):
    base = 128 * k
    row = base + 8 * p
    sub = lax.broadcasted_iota(jnp.int32, (8, 128), 0)
    lane = lax.broadcasted_iota(jnp.int32, (8, 128), 1)

    def load(q):
        return [a[base + 8 * q:base + 8 * q + 8, base + 128 * t:base + 128 * t + 128] for t in range(tiles)]

    rows = load(p)
    if p == 0:
        spread = [lane_spread(rows[0], j) for j in range(8)]
    spread = list(spread)
    near = range(p + 1, min(p + 4, 16))
    groups = {q: load(q) for q in near}
    columns = {q: [lane_spread(groups[q][0], 8 * p + c) for c in range(8)] for q in near}
    done = [[] for _ in range(tiles)]
    for i in range(8):
        s = lax.rsqrt(row_spread(spread[i], i))
        u = spread[i] * s
        for q in near:
            columns[q][i] = columns[q][i] * s
        for j in range(i + 1, 8):
            f = row_spread(u, j)
            spread[j] = spread[j] - u * f
            for q in near:
                columns[q][j] = columns[q][j] - f * columns[q][i]
        for t in range(tiles):
            final = row_spread(rows[t], i) * s
            done[t].append(final)
            if i < 7:
                rows[t] = rows[t] - u * final
    for t in range(tiles):
        val = done[t][0]
        for i in range(1, 8):
            val = jnp.where(sub == i, done[t][i], val)
        if t == 0:
            new = val
            val = jnp.where(lane >= 8 * p + sub, val, 0.0)
        out[row:row + 8, base + 128 * t:base + 128 * t + 128] = val
    if p == 15:
        return None
    first = columns[p + 1]
    ahead = []
    for c in range(8):
        total = tree(first[i] * row_spread(first[i], c) for i in range(8))
        ahead.append(lane_spread(groups[p + 1][0], 8 * (p + 1) + c) - total)
    turned = jnp.transpose(new) if p < 12 else None
    for q in range(p + 1, 16):
        if q in near:
            g, h = groups[q], columns[q]
        else:
            g = load(q)
            h = [jnp.broadcast_to(turned[8 * q:8 * q + 8, i:i + 1], (8, 128)) for i in range(8)]
        for t in range(tiles):
            a[base + 8 * q:base + 8 * q + 8, base + 128 * t:base + 128 * t + 128] = g[t] - tree(h[i] * done[t][i] for i in range(8))
    return ahead


def factor_kernel(index_ref, packed_ref, out, a):
    n = a.shape[0]
    out[...] = jnp.zeros((n, n), jnp.float32)
    degree = index_ref[0:1, :].astype(jnp.float32)
    kaula = kaula_gain * (degree / NMAX) ** 2
    diagonal = lax.broadcasted_iota(jnp.int32, (LANES, LANES), 0) == lax.broadcasted_iota(jnp.int32, (LANES, LANES), 1)
    for at, (i, j) in enumerate(UPPER):
        block = packed_ref[at * LANES:(at + 1) * LANES, :]
        if i == j:
            weight = kaula[:, i * LANES:(i + 1) * LANES]
            block = block + jnp.where(diagonal, weight * weight, 0.0)
        a[i * LANES:(i + 1) * LANES, j * LANES:(j + 1) * LANES] = block
    for k in range(TILE_BLOCKS):
        ahead = None
        for p in range(16):
            ahead = panel(a, out, k, p, TILE_BLOCKS - k, ahead)
        done = slice(k * LANES, (k + 1) * LANES)
        for i in range(k + 1, TILE_BLOCKS):
            left = out[done, i * LANES:(i + 1) * LANES]
            a[i * LANES:(i + 1) * LANES, i * LANES:] -= lax.dot_general(
                left, out[done, i * LANES:], (((0,), (0,)), ((), ())), precision=highest,
                preferred_element_type=jnp.float32)


def upper_factor(packed, column_index):
    n = column_index.shape[1]
    return pl.pallas_call(
        factor_kernel,
        out_shape=jax.ShapeDtypeStruct((n, n), jnp.float32),
        in_specs=[pl.BlockSpec(memory_space=pltpu.VMEM)] * 2,
        out_specs=pl.BlockSpec(memory_space=pltpu.VMEM),
        scratch_shapes=[pltpu.VMEM((n, n), jnp.float32)],
        compiler_params=pltpu.CompilerParams(vmem_limit_bytes=16 * 2**20),
        name="upper_factor",
    )(column_index, packed)


def body(legendre, lon_center, counts, column_index):
    packed = panel_gram(legendre, lon_center, counts, column_index)
    return upper_factor(packed, column_index)


def solution(mesh):
    placed = (P("ord", "grp"), P("grp"), P("grp", None), P())
    return jax.shard_map(body, mesh=mesh, in_specs=placed, out_specs=P(), check_vma=False)
```

```python
import math

import jax
import jax.numpy as jnp
import numpy as np
from jax import lax
from jax.experimental import pallas as pl
from jax.experimental.pallas import tpu as pltpu
from jax.sharding import PartitionSpec as P

NMAX = 120

track_span = 0.3
kaula_gain = 1.2
highest = lax.Precision.HIGHEST
by_mesh = pl.DeviceIdType.MESH

LANES = 128
TILE_BLOCKS = 4
UPPER = [(i, j) for i in range(TILE_BLOCKS) for j in range(i, TILE_BLOCKS)]

CHIP_OFFSETS = [
    (2, 2), (2, 1), (1, 2), (2, 3), (3, 2), (2, 0), (0, 2), (1, 1), (3, 3), (1, 3), (3, 1),
    (1, 0), (0, 1), (3, 0), (0, 3),
]
OFFSETS = [(dx, dy, dc) for dc in (0, 1) for dx, dy in CHIP_OFFSETS] + [(0, 0, 1)]
DEPTHS = (4, 3, 5, 2, 6, 1, 7)
SPANS = (24, 16)


def sine_terms():
    g = np.cos(np.linspace(0.0, np.pi / 2, 400)) * 0.25
    g = g[g > 1e-4]
    powers = np.stack([g ** (2 * k + 1) for k in range(6)], axis=1)
    return [float(c) for c in np.linalg.lstsq(powers, np.sin(2 * np.pi * g), rcond=None)[0]]


SINE = sine_terms()


def remote(src, dst, sems, index, device):
    return pltpu.make_async_remote_copy(src_ref=src, dst_ref=dst, send_sem=sems[0].at[index], recv_sem=sems[1].at[index],
                                        device_id=device, device_id_type=by_mesh)


def reduce_everywhere(me, depth, packed, other, part, plane, piece, total, *sems):
    pair_sems, sems1, sems2, sems3, sems4 = [sems[2 * k:2 * k + 2] for k in range(5)]
    x, y, core = me // 8, (me // 2) % 4, me % 2
    partner = me + 1 - 2 * core
    chip = me // 2
    chips = [((x + dx) % 4) * 4 + (y + dy) % 4 for dx, dy in CHIP_OFFSETS]
    layers = [(depth + d) % 8 for d in DEPTHS]
    half_rows = other.shape[0]
    spans, at = [], 0
    for n in SPANS:
        spans.append((at, n))
        at += n
    def at_half(c, start, n):
        return pl.ds(pl.multiple_of(c * half_rows + start, 8), n)
    pair = []
    for s, (a, n) in enumerate(spans):
        pair.append(remote(packed.at[at_half(1 - core, a * 16, n * 16)], other.at[pl.ds(a * 16, n * 16)], pair_sems, s, {"ord": partner}))
    for copy in pair:
        copy.start()
    def rows(c, a, n):
        return a * 16 + c * n
    first, second, third, fourth = [], [], [], []
    for s, (a, n) in enumerate(spans):
        pair[s].wait_recv()
        mine = at_half(core, a * 16, n * 16)
        packed[mine, :] = packed[mine, :] + other[pl.ds(a * 16, n * 16), :]
        step = [remote(packed.at[at_half(core, rows(c, a, n), n)], part.at[j, pl.ds(a, n)], sems1, (s, j), {"ord": c * 2 + core}) for j, c in enumerate(chips)]
        for copy in step:
            copy.start()
        first.append(step)
    for s, (a, n) in enumerate(spans):
        value = packed[at_half(core, rows(chip, a, n), n), :]
        for j, copy in enumerate(first[s]):
            copy.wait_recv()
            value = value + part[j, pl.ds(a, n), :]
        plane[depth, pl.ds(a, n), :] = value
        step = [remote(plane.at[depth, pl.ds(a, n)], plane.at[depth, pl.ds(a, n)], sems2, (s, j), {"grp": l}) for j, l in enumerate(layers)]
        for copy in step:
            copy.start()
        second.append(step)
    for s, (a, n) in enumerate(spans):
        for copy in second[s]:
            copy.wait_recv()
        value = plane[0, pl.ds(a, n), :]
        for d in range(1, 8):
            value = value + plane[d, pl.ds(a, n), :]
        piece[pl.ds(a, n), :] = value
        home = at_half(core, rows(chip, a, n), n)
        step = [remote(piece.at[pl.ds(a, n)], total.at[home], sems3, (s, j), {"ord": c * 2 + core}) for j, c in enumerate(chips)]
        for copy in step:
            copy.start()
        third.append(step)
        keep = remote(piece.at[pl.ds(a, n)], total.at[home], sems4, (s, 15), {"ord": partner})
        keep.start()
        fourth.append([keep])
        total[home, :] = value
    back = [((x - dx) % 4) * 4 + (y - dy) % 4 for dx, dy in CHIP_OFFSETS]
    for s, (a, n) in enumerate(spans):
        for j in reversed(range(15)):
            third[s][j].wait_recv()
            spot = total.at[at_half(core, rows(back[j], a, n), n)]
            copy = remote(spot, spot, sems4, (s, j), {"ord": partner})
            copy.start()
            fourth[s].append(copy)
    for s in range(len(spans)):
        for copy in fourth[s]:
            copy.wait_recv()
    return pair + [c for group in first + second + third + fourth for c in group]


def tiles_in(count):
    return lax.shift_right_logical(count + (LANES - 1), 7)


def compact_kernel(counts_ref, legendre_ref, out_ref, sem):
    segments = counts_ref.shape[1]
    per_segment = legendre_ref.shape[1] // segments // LANES
    sizes = [1 << b for b in reversed(range(per_segment.bit_length()))]

    def span(at, size):
        return pl.ds(pl.multiple_of(at * LANES, LANES), size * LANES)

    def segment(k, to):
        n = tiles_in(counts_ref[0, k])
        at = k * per_segment
        for size in sizes:
            has = (n & size) != 0

            @pl.when(has)
            def _(at=at, to=to, size=size):
                pltpu.make_async_copy(legendre_ref.at[:, span(at, size)], out_ref.at[:, span(to, size)], sem).start()

            step = jnp.where(has, size, 0)
            at, to = at + step, to + step
        return to

    moved = lax.fori_loop(0, segments, segment, jnp.int32(0))
    for b in reversed(range((out_ref.shape[1] // LANES).bit_length())):
        @pl.when((moved & (1 << b)) != 0)
        def _(b=b):
            whole = pl.ds(0, LANES << b)
            pltpu.make_async_copy(legendre_ref.at[:, whole], out_ref.at[:, whole], sem).wait()


def compact(legendre, counts, lanes):
    return pl.pallas_call(
        compact_kernel,
        out_shape=jax.ShapeDtypeStruct((legendre.shape[0], lanes), jnp.float32),
        in_specs=[pl.BlockSpec(memory_space=pltpu.SMEM), pl.BlockSpec(memory_space=pltpu.HBM)],
        out_specs=pl.BlockSpec(memory_space=pltpu.VMEM),
        scratch_shapes=[pltpu.SemaphoreType.DMA],
        compiler_params=pltpu.CompilerParams(vmem_limit_bytes=44 * 2**20),
        name="compact",
    )(counts, legendre)


def gram_kernel(rows_grp, lon_ref, counts_ref, index_ref, own_ref, out_ref,
                starts, tile_at, filled, order, first, got, got_last, high, low, packed, other, part, plane, piece, total,
                own_sem, send_sem, recv_sem, *step_sems):
    me = lax.axis_index("ord")
    depth = lax.axis_index("grp")
    segments = counts_ref.shape[1]
    per_segment = rows_grp // segments // LANES
    chunks, _, cols, lanes = got.shape
    width = lanes // LANES
    total_cols = segments * cols
    x, y, core = me // 8, (me // 2) % 4, me % 2

    def neighbour(offset):
        dx, dy, dc = offset
        return ((x + dx) % 4) * 8 + ((y + dy) % 4) * 2 + (core + dc) % 2

    peers = [neighbour(o) for o in OFFSETS]
    layers = [(depth + d) % 8 for d in DEPTHS]

    barrier = pltpu.get_barrier_semaphore()
    for peer in peers:
        pl.semaphore_signal(barrier, inc=1, device_id={"ord": peer}, device_id_type=by_mesh)
    for layer in layers:
        pl.semaphore_signal(barrier, inc=1, device_id={"grp": layer}, device_id_type=by_mesh)
    pl.semaphore_wait(barrier, len(peers) + len(layers))

    def own_tiles(c, d):
        return own_ref.at[:, pl.ds(pl.multiple_of((c * segments + d) * lanes, LANES), lanes)]

    def last_tile(d):
        return own_ref.at[:, pl.ds(pl.multiple_of(chunks * segments * lanes + d * LANES, LANES), LANES)]

    def send(src, dst, c, j):
        return pltpu.make_async_remote_copy(
            src_ref=src, dst_ref=dst, send_sem=send_sem.at[c, j], recv_sem=recv_sem.at[c, j],
            device_id={"ord": peers[j]}, device_id_type=by_mesh)

    def chunk_copies(c):
        return [send(own_tiles(c, peers[j]), got.at[c, me], c, j) for j in range(len(peers))]

    last_copies = [send(last_tile(peers[j]), got_last.at[me], chunks, j) for j in range(len(peers))]

    def own_copy(c):
        return pltpu.make_async_copy(own_tiles(c, me), got.at[c, me], own_sem.at[c])

    own_last = pltpu.make_async_copy(last_tile(me), got_last.at[me], own_sem.at[chunks])

    def send_chunk(c, carry):
        for copy in chunk_copies(c):
            copy.start()
        own_copy(c).start()
        return carry

    lax.fori_loop(0, chunks, send_chunk, 0)
    for copy in last_copies:
        copy.start()
    own_last.start()

    begin = jnp.int32(0)
    for k in range(segments):
        starts[k] = begin
        begin = begin + tiles_in(counts_ref[0, k])

    def list_tile(t, carry):
        at = (t // width * segments + me) * width + t % width
        at = jnp.where(t < chunks * width, at, chunks * segments * width + me)
        tile, left = jnp.int32(0), jnp.int32(0)
        for k in range(segments):
            step = at - starts[k]
            left_here = counts_ref[0, k] - step * LANES
            inside = jnp.logical_and(step >= 0, left_here > 0)
            tile = jnp.where(inside, k * per_segment + step, tile)
            left = jnp.where(inside, left_here, left)
        tile_at[t] = tile
        filled[t] = left
        return carry

    lax.fori_loop(0, chunks * width + 1, list_tile, 0)

    rate = track_span / rows_grp / (2 * math.pi)
    start = lon_ref[0] * (1.0 / (2 * math.pi))
    for i in range(TILE_BLOCKS):
        mine = slice(i * LANES, (i + 1) * LANES)

        def down(row):
            return jnp.transpose(jnp.broadcast_to(index_ref[row:row + 1, mine], (LANES, LANES)).astype(jnp.float32))

        m = down(1)
        base = m * start - 0.25 * down(2)
        base = base - jnp.floor(base + 0.5)
        order[mine, :] = m
        first[mine, :] = base + m * (rate * lax.broadcasted_iota(jnp.int32, (LANES, LANES), 1).astype(jnp.float32))
    scale = 1.0 / math.sqrt(rows_grp * lax.axis_size("grp"))
    packed[...] = jnp.zeros_like(packed)

    def product(left, right):
        return lax.dot_general(left, right, (((1,), (1,)), ((), ())), preferred_element_type=jnp.float32)

    def add_tiles(tiles_ref, first_tile, count_tiles):
        for i in range(count_tiles):
            t = first_tile + i
            shift = tile_at[t].astype(jnp.float32) * (rate * LANES)
            count = filled[t]
            part_lanes = slice(i * LANES, (i + 1) * LANES)

            def wave_rows(r, carry):
                rows = pl.ds(pl.multiple_of(r * 64, 64), 64)
                values = tiles_ref[pl.ds(r * (64 // cols), 64 // cols), :, part_lanes].reshape(64, LANES)
                turns = first[rows, :] + order[rows, :] * shift
                turns = turns - jnp.floor(turns + 0.5)
                g = 0.25 - jnp.abs(turns)
                z = g * g
                wave = jnp.full_like(z, SINE[-1] * scale)
                for term in SINE[-2::-1]:
                    wave = wave * z + term * scale
                lane = lax.broadcasted_iota(jnp.int32, (64, LANES), 1)
                values = jnp.where(lane < count, values * (wave * g), 0.0)
                upper = values.astype(jnp.bfloat16)
                high[rows, part_lanes] = upper
                low[rows, part_lanes] = (values - upper.astype(jnp.float32)).astype(jnp.bfloat16)
                return carry

            lax.fori_loop(0, total_cols // 64, wave_rows, 0)
        depth_lanes = slice(0, count_tiles * LANES)
        at = 0
        for i in range(TILE_BLOCKS):
            mine = slice(i * LANES, (i + 1) * LANES)
            rest = slice(i * LANES, total_cols)
            gram = product(high[mine, depth_lanes], high[rest, depth_lanes])
            gram += product(high[mine, depth_lanes], low[rest, depth_lanes])
            gram += product(low[mine, depth_lanes], high[rest, depth_lanes])
            for k in range(TILE_BLOCKS - i):
                packed[at * LANES:(at + 1) * LANES, :] += gram[:, k * LANES:(k + 1) * LANES]
                at += 1

    def add_chunk(c, carry):
        for copy in chunk_copies(c):
            copy.wait_recv()
        own_copy(c).wait()
        add_tiles(got.at[c], c * width, width)
        return carry

    lax.fori_loop(0, chunks, add_chunk, 0)
    for copy in last_copies:
        copy.wait_recv()
    own_last.wait()
    add_tiles(got_last, chunks * width, 1)

    sends = reduce_everywhere(me, depth, packed, other, part, plane, piece, total, *step_sems)
    out_ref[...] = total[...]
    for copy in sends:
        copy.wait_send()

    def drain(c, carry):
        for copy in chunk_copies(c):
            copy.wait_send()
        return carry

    lax.fori_loop(0, chunks, drain, 0)
    for copy in last_copies:
        copy.wait_send()


def panel_gram(legendre, lon_center, counts, column_index):
    cols, rows_grp = legendre.shape
    segments = counts.shape[1]
    total_cols = column_index.shape[1]
    tiles = (rows_grp * 3 // 4) // LANES + segments
    per_device = -(-tiles // segments)
    width = 6
    chunks = (per_device - 1) // width
    assert chunks * width + 1 == per_device
    packed_rows = len(UPPER) * LANES
    share = packed_rows // segments
    peers, layers = len(OFFSETS), len(DEPTHS)
    f32 = jnp.float32
    dma = pltpu.SemaphoreType.DMA
    own = compact(legendre, counts, segments * per_device * LANES)
    return pl.pallas_call(
        lambda *refs: gram_kernel(rows_grp, *refs),
        out_shape=jax.ShapeDtypeStruct((packed_rows, LANES), f32),
        in_specs=[
            pl.BlockSpec(memory_space=pltpu.SMEM),
            pl.BlockSpec(memory_space=pltpu.SMEM),
            pl.BlockSpec(memory_space=pltpu.VMEM),
            pl.BlockSpec(memory_space=pl.ANY),
        ],
        out_specs=pl.BlockSpec(memory_space=pltpu.VMEM),
        scratch_shapes=[
            pltpu.SMEM((segments,), jnp.int32),
            pltpu.SMEM((per_device,), jnp.int32),
            pltpu.SMEM((per_device,), jnp.int32),
            pltpu.VMEM((total_cols, LANES), f32),
            pltpu.VMEM((total_cols, LANES), f32),
            pltpu.VMEM((chunks, segments, cols, width * LANES), f32),
            pltpu.VMEM((segments, cols, LANES), f32),
            pltpu.VMEM((total_cols, width * LANES), jnp.bfloat16),
            pltpu.VMEM((total_cols, width * LANES), jnp.bfloat16),
            pltpu.VMEM((packed_rows, LANES), f32),
            pltpu.VMEM((packed_rows // 2, LANES), f32),
            pltpu.VMEM((len(CHIP_OFFSETS), share, LANES), f32),
            pltpu.VMEM((layers + 1, share, LANES), f32),
            pltpu.VMEM((share, LANES), f32),
            pltpu.VMEM((packed_rows, LANES), f32),
            dma((chunks + 1,)),
            dma((chunks + 1, peers)), dma((chunks + 1, peers)),
            dma((len(SPANS),)), dma((len(SPANS),)),
            dma((len(SPANS), len(CHIP_OFFSETS))), dma((len(SPANS), len(CHIP_OFFSETS))),
            dma((len(SPANS), layers)), dma((len(SPANS), layers)),
            dma((len(SPANS), len(CHIP_OFFSETS))), dma((len(SPANS), len(CHIP_OFFSETS))),
            dma((len(SPANS), len(CHIP_OFFSETS) + 1)), dma((len(SPANS), len(CHIP_OFFSETS) + 1)),
        ],
        compiler_params=pltpu.CompilerParams(collective_id=0, has_side_effects=True, vmem_limit_bytes=24 * 2**20),
        name="panel_gram",
    )(lon_center, counts, column_index, own)


def lane_spread(v, j):
    return jnp.broadcast_to(v[:, j:j + 1], (8, 128))


def row_spread(v, i):
    return jnp.broadcast_to(v[i:i + 1, :], (8, 128))


def tree(terms):
    terms = list(terms)
    while len(terms) > 1:
        terms = [terms[i] + terms[i + 1] if i + 1 < len(terms) else terms[i] for i in range(0, len(terms), 2)]
    return terms[0]


def panel(a, out, k, p, tiles, spread):
    base = 128 * k
    row = base + 8 * p
    sub = lax.broadcasted_iota(jnp.int32, (8, 128), 0)
    lane = lax.broadcasted_iota(jnp.int32, (8, 128), 1)

    def load(q):
        return [a[base + 8 * q:base + 8 * q + 8, base + 128 * t:base + 128 * t + 128] for t in range(tiles)]

    rows = load(p)
    if p == 0:
        spread = [lane_spread(rows[0], j) for j in range(8)]
    spread = list(spread)
    near = range(p + 1, min(p + 4, 16))
    groups = {q: load(q) for q in near}
    columns = {q: [lane_spread(groups[q][0], 8 * p + c) for c in range(8)] for q in near}
    done = [[] for _ in range(tiles)]
    for i in range(8):
        s = lax.rsqrt(row_spread(spread[i], i))
        u = spread[i] * s
        for q in near:
            columns[q][i] = columns[q][i] * s
        for j in range(i + 1, 8):
            f = row_spread(u, j)
            spread[j] = spread[j] - u * f
            for q in near:
                columns[q][j] = columns[q][j] - f * columns[q][i]
        for t in range(tiles):
            final = row_spread(rows[t], i) * s
            done[t].append(final)
            if i < 7:
                rows[t] = rows[t] - u * final
    for t in range(tiles):
        val = done[t][0]
        for i in range(1, 8):
            val = jnp.where(sub == i, done[t][i], val)
        if t == 0:
            new = val
            val = jnp.where(lane >= 8 * p + sub, val, 0.0)
        out[row:row + 8, base + 128 * t:base + 128 * t + 128] = val
    if p == 15:
        return None
    first = columns[p + 1]
    ahead = []
    for c in range(8):
        total = tree(first[i] * row_spread(first[i], c) for i in range(8))
        ahead.append(lane_spread(groups[p + 1][0], 8 * (p + 1) + c) - total)
    turned = jnp.transpose(new) if p < 12 else None
    for q in range(p + 1, 16):
        if q in near:
            g, h = groups[q], columns[q]
        else:
            g = load(q)
            h = [jnp.broadcast_to(turned[8 * q:8 * q + 8, i:i + 1], (8, 128)) for i in range(8)]
        for t in range(tiles):
            a[base + 8 * q:base + 8 * q + 8, base + 128 * t:base + 128 * t + 128] = g[t] - tree(h[i] * done[t][i] for i in range(8))
    return ahead


def factor_kernel(index_ref, packed_ref, out, a):
    n = a.shape[0]
    out[...] = jnp.zeros((n, n), jnp.float32)
    degree = index_ref[0:1, :].astype(jnp.float32)
    kaula = kaula_gain * (degree / NMAX) ** 2
    diagonal = lax.broadcasted_iota(jnp.int32, (LANES, LANES), 0) == lax.broadcasted_iota(jnp.int32, (LANES, LANES), 1)
    for at, (i, j) in enumerate(UPPER):
        block = packed_ref[at * LANES:(at + 1) * LANES, :]
        if i == j:
            weight = kaula[:, i * LANES:(i + 1) * LANES]
            block = block + jnp.where(diagonal, weight * weight, 0.0)
        a[i * LANES:(i + 1) * LANES, j * LANES:(j + 1) * LANES] = block
    for k in range(TILE_BLOCKS):
        ahead = None
        for p in range(16):
            ahead = panel(a, out, k, p, TILE_BLOCKS - k, ahead)
        done = slice(k * LANES, (k + 1) * LANES)
        for i in range(k + 1, TILE_BLOCKS):
            left = out[done, i * LANES:(i + 1) * LANES]
            a[i * LANES:(i + 1) * LANES, i * LANES:] -= lax.dot_general(
                left, out[done, i * LANES:], (((0,), (0,)), ((), ())), precision=highest,
                preferred_element_type=jnp.float32)


def upper_factor(packed, column_index):
    n = column_index.shape[1]
    return pl.pallas_call(
        factor_kernel,
        out_shape=jax.ShapeDtypeStruct((n, n), jnp.float32),
        in_specs=[pl.BlockSpec(memory_space=pltpu.VMEM)] * 2,
        out_specs=pl.BlockSpec(memory_space=pltpu.VMEM),
        scratch_shapes=[pltpu.VMEM((n, n), jnp.float32)],
        compiler_params=pltpu.CompilerParams(vmem_limit_bytes=16 * 2**20),
        name="upper_factor",
    )(column_index, packed)


def body(legendre, lon_center, counts, column_index):
    packed = panel_gram(legendre, lon_center, counts, column_index)
    return upper_factor(packed, column_index)


def solution(mesh):
    placed = (P("ord", "grp"), P("grp"), P("grp", None), P())
    return jax.shard_map(body, mesh=mesh, in_specs=placed, out_specs=P(), check_vma=False)
```
